256 devices in a mesh: lon: 64 (over x_hi, z, y), lat: 4 (over x_lo, core).
Axes of the slice: x: 4 (x_hi: 2, x_lo: 2; x = x_hi * 2 + x_lo), y: 4, z: 8, core: 2. Of those that a mesh axis runs over, the one named last changes fastest.
Arguments:
- height: float32 [256, 16000], P('lat', 'lon'), may hold values from -6 to 6
- divergence: float32 [256, 16000], P('lat', 'lon'), may hold values from -6 to 6
- depth: float32 [256, 16000], P('lat', 'lon'), may hold values from 0.25 to 4
- tide: float32 [256, 16000], P('lat', 'lon'), may hold values from -6 to 6
- gauss_weight: float32 [128], P('lat'), may hold values from 0.5 to 1.5
- legendre: bfloat16 [1792, 128, 3585], P('lon', 'lat'), may hold values from -4 to 4
Outputs:
- height_new: float32 [256, 16000], P('lat', 'lon')
- divergence_new: float32 [256, 16000], P('lat', 'lon')
The draws below stay inside these ranges and needn't reach their ends.
All inputs are finite; a program needn't handle non-finite values.
Results may differ from the reference program's by a relative error of at most 0.0032.
Values may be sent and summed in bfloat16 or wider, within the bound.
A program may use at most 128 MiB of HBM per device.

```python
import math
import jax
import jax.numpy as jnp
from jax import lax

NLON = 16000
PAIRS_DEV = 28
LAT_HALF = 32
MT = 3584
K = 3585
NLAT = 256
N_LON = 64
N_LAT = 4


def levels(own_key, dims, shards, low, high):
    factor_of, own = 1.0, jax.random.fold_in(own_key, 6)
    for axis_at, blocks in shards:
        draws = jnp.exp(jax.random.uniform(jax.random.fold_in(own, axis_at), (blocks,), jnp.float32, low / len(shards), high / len(shards)))
        factor_of = factor_of * jnp.repeat(draws, dims[axis_at] // blocks).reshape([-1 if axis == axis_at else 1 for axis in range(len(dims))])
    return factor_of


def normal_values(stream_key, dims, width, reach, shards=(), held_as=jnp.bfloat16):
    factor_of = levels(stream_key, dims, shards, -0.22, 0.18) if shards else 1.0
    array = jax.random.normal(stream_key, dims, jnp.float32) * width * factor_of
    return jnp.minimum(jnp.maximum(array, -reach), reach).astype(held_as)


def setup_inputs(seed: int = 0) -> dict:
    key_of = jax.random.split(jax.random.key(seed), 7)
    return {
        "height": normal_values(key_of[0], (NLAT, NLON), 1.0, 6.0, ((0, 4), (1, 64)), jnp.float32),
        "divergence": normal_values(key_of[1], (NLAT, NLON), 1.0, 6.0, ((0, 4), (1, 64)), jnp.float32),
        "depth": jnp.clip(jnp.exp(math.log(4.0) - 2.7725887 * jax.random.uniform(key_of[2], (NLAT, NLON), jnp.float32) ** levels(key_of[2], (NLAT, NLON), ((0, 4), (1, 64)), -0.2, 0.2)), 0.25, 4.0),
        "tide": normal_values(key_of[3], (NLAT, NLON), 1.0, 6.0, ((0, 4), (1, 64)), jnp.float32),
        "gauss_weight": jnp.clip(0.5 + 1.0 * jax.random.uniform(key_of[4], (LAT_HALF * N_LAT,), jnp.float32) ** levels(key_of[4], (LAT_HALF * N_LAT,), ((0, 4),), -0.2, 0.2), 0.5, 1.5),
        "legendre": normal_values(key_of[5], (MT // 2, LAT_HALF * N_LAT, K), 1.0, 4.0, ((0, 64), (1, 4))),
    }


time_step = 0.5
drag_step = 0.1
coupling = 2.0
gravity_step = 4.0

def slot_layout(pair_first, pair_count, wave_count, slot_count):
    pair_index = pair_first + jnp.arange(pair_count, dtype=jnp.int32)
    slot_index = jnp.arange(slot_count, dtype=jnp.int32)[None, :]
    pair_column = pair_index[:, None]
    upper_slot = slot_index >= wave_count - pair_column
    degree = jnp.where(upper_slot, slot_index - 1, pair_column + slot_index)
    parity = jnp.where(upper_slot, (slot_index + pair_column + wave_count) % 2, slot_index % 2)
    eigen_value = degree.astype(jnp.float32) * (degree + 1).astype(jnp.float32) / float(wave_count * wave_count)
    return (upper_slot, parity, eigen_value)

def helmholtz(height_rhs, div_rhs, eigen_value):
    height_spec = (height_rhs - time_step * div_rhs) / (1.0 + coupling * eigen_value)
    div_spec = div_rhs + gravity_step * eigen_value * height_spec
    return jnp.stack([height_spec, div_spec]).astype(jnp.bfloat16)

def forward_pair(operands):
    table, lower_cols, upper_cols, upper_slot, parity = operands
    both_cols = jnp.stack([lower_cols, upper_cols]).astype(jnp.float32)
    lat_sums = jnp.einsum('jk,afqrj->afqrk', table.astype(jnp.float32), both_cols)
    odd_slot = parity == 1
    pick_lower = jnp.where(odd_slot, lat_sums[0][:, 1], lat_sums[0][:, 0])
    pick_upper = jnp.where(odd_slot, lat_sums[1][:, 1], lat_sums[1][:, 0])
    return jnp.where(upper_slot, pick_upper, pick_lower)

def inverse_pair(operands):
    table, solved_pair, upper_slot, parity = operands
    member_masks = jnp.stack([jnp.logical_not(upper_slot), upper_slot]).astype(jnp.float32)
    parity_masks = jnp.stack([parity == 0, parity == 1]).astype(jnp.float32)
    masked = solved_pair.astype(jnp.float32)[None, None] * member_masks[:, None, None, None, :] * parity_masks[None, :, None, None, :]
    lat_sums = jnp.einsum('jk,aqfrk->aqfrj', table.astype(jnp.float32), masked)
    north_part = lat_sums[:, 0] + lat_sums[:, 1]
    south_part = lat_sums[:, 0] - lat_sums[:, 1]
    return jnp.stack([north_part, south_part])

def reference(height, divergence, depth, tide, gauss_weight, legendre):
    wave_count = 2 * PAIRS_DEV * N_LON
    half_count = wave_count // 2
    slot_count = wave_count + 1
    lat_count = 2 * LAT_HALF * N_LAT
    north_count = LAT_HALF * N_LAT
    norm_factor = math.sqrt(NLON / lat_count) / wave_count
    forcing = jnp.stack([height - time_step * (depth - 1.0) * divergence, divergence * (1.0 - drag_step / depth), tide])
    spectrum = jnp.fft.rfft(forcing, axis=-1)[:, :, :wave_count]
    lon_scale = 1.0 / NLON
    fourier = jnp.stack([jnp.real(spectrum), jnp.imag(spectrum)], axis=1).astype(jnp.float32) * lon_scale
    band_form = fourier.reshape(3, 2, N_LAT, 2, LAT_HALF, wave_count)
    north_part = band_form[:, :, :, 0].reshape(3, 2, north_count, wave_count)
    south_part = band_form[:, :, :, 1].reshape(3, 2, north_count, wave_count)
    weight = (gauss_weight * norm_factor)[None, None, :, None]
    even_part = (north_part + south_part) * weight
    odd_part = (north_part - south_part) * weight
    folded = jnp.stack([even_part, odd_part], axis=1).astype(jnp.bfloat16)
    lower_cols = jnp.moveaxis(folded[..., :half_count], -1, 0)
    upper_cols = jnp.moveaxis(folded[..., ::-1][..., :half_count], -1, 0)
    upper_slot, parity, eigen_value = slot_layout(0, half_count, wave_count, slot_count)
    spectral = lax.map(forward_pair, (legendre, lower_cols, upper_cols, upper_slot, parity))
    spectral = jnp.moveaxis(spectral, 0, 2)
    div_rhs = spectral[1] - gravity_step * eigen_value * spectral[2]
    solved = helmholtz(spectral[0], div_rhs, eigen_value)
    lat_values = lax.map(inverse_pair, (legendre, jnp.moveaxis(solved, 2, 0), upper_slot, parity))
    lower_waves = lat_values[:, :, 0]
    upper_waves = lat_values[:, :, 1][::-1]
    coefficients = jnp.concatenate([lower_waves, upper_waves], axis=0)
    coefficients = coefficients.reshape(wave_count, 2, 2, 2, N_LAT, LAT_HALF)
    coefficients = jnp.transpose(coefficients, (2, 3, 4, 1, 5, 0)).reshape(2, 2, lat_count, wave_count)
    complex_waves = coefficients[:, 0] + 1j * coefficients[:, 1]
    padded = jnp.pad(complex_waves, ((0, 0), (0, 0), (0, NLON // 2 + 1 - wave_count)))
    new_fields = jnp.fft.irfft(padded, n=NLON, axis=-1) * NLON
    return (new_fields[0].astype(jnp.float32), new_fields[1].astype(jnp.float32))
```

```python
import math

import jax
import jax.numpy as jnp
import ml_dtypes
import numpy as np
from jax import lax
from jax.experimental import pallas as pl
from jax.experimental.pallas import tpu as pltpu
from jax.sharding import PartitionSpec as P

time_step = 0.5
drag_step = 0.1
coupling = 2.0
gravity_step = 4.0

f32, bf16 = jnp.float32, jnp.bfloat16

LON_DEV = 64
SPAN = 250
NLON = LON_DEV * SPAN
PAIRS = 28
MT = 2 * PAIRS * LON_DEV
SLOTS = MT + 1
HALF = 32
NLAT = 256
GROUP = 4
GROUPS = PAIRS // GROUP
TILE = 512
TILES = (SLOTS - 1) // TILE
WIDE = 3840
PART = WIDE // 2


def two_terms(table):
    high = table.astype(ml_dtypes.bfloat16)
    low = (table - high.astype(np.float64)).astype(ml_dtypes.bfloat16)
    return high, low


def tables():
    v = np.arange(128)
    s = np.arange(LON_DEV)
    j = np.arange(256)
    real = (j < SPAN).astype(np.float64)
    tau = np.arange(16)
    first = np.stack([v, MT - 1 - v])
    turn = np.stack([128 * tau, -128 * tau])
    psi = 2 * np.pi * ((first[:, :, None] * s) % LON_DEV) / LON_DEV
    spread = np.stack([np.cos(psi), -np.sin(psi)], axis=1).reshape(512, LON_DEV)
    theta = 2 * np.pi * ((first[:, :, None] * j) % NLON) / NLON
    twist_cos = (np.cos(theta) * real).reshape(256, 256).astype(np.float32)
    twist_sin = (np.sin(theta) * real).reshape(256, 256).astype(np.float32)
    phi = 2 * np.pi * ((turn[:, :, None] * j) % NLON) / NLON
    keep = real * (tau < 14)[:, None]
    cos, sin = np.cos(phi) * keep, np.sin(phi) * keep
    inner = np.concatenate(
        [np.concatenate([cos, sin], axis=2), np.concatenate([-sin, cos], axis=2)], axis=1
    ).reshape(64, 512)
    row = (PAIRS * s) // 128
    pick = np.concatenate([row[:, None] == tau, row[:, None] + 1 == tau]).astype(np.float64)
    back_row = np.concatenate([row, row + 1])
    back_phi = np.stack([back_row, -back_row])[:, :, None] * 128 * j % NLON * (2 * np.pi / NLON)
    cos, sin = 2 * np.cos(back_phi) * real, 2 * np.sin(back_phi) * real
    back = np.concatenate(
        [np.concatenate([cos, sin], axis=2), np.concatenate([-sin, cos], axis=2)], axis=1
    ).reshape(512, 512)
    return (
        *two_terms(spread),
        *two_terms(np.ascontiguousarray(spread.T)),
        twist_cos,
        twist_sin,
        *two_terms(inner),
        pick.astype(ml_dtypes.bfloat16),
        *two_terms(back),
    )


def iota(shape, dim):
    return lax.broadcasted_iota(jnp.int32, shape, dim)


def dot(a, b):
    return lax.dot_general(a, b, (((1,), (0,)), ((), ())), preferred_element_type=f32)


def dot_nt(a, b):
    return lax.dot_general(a, b, (((1,), (1,)), ((), ())), preferred_element_type=f32)


def split(x):
    high = x.astype(bf16)
    return high, (x - high.astype(f32)).astype(bf16)


def three(product, a, b):
    return product(a[0], b[0]) + (product(a[0], b[1]) + product(a[1], b[0]))


def forcing_fields(height, divergence, depth, tide):
    return (
        height - time_step * (depth - 1.0) * divergence,
        divergence * (1.0 - drag_step / depth),
        tide,
    )


def fold(field, weight):
    north, south = field[:HALF], field[HALF:]
    return (north + south) * weight, (north - south) * weight


def lane_masks():
    lane = iota((LON_DEV, 128), 1)
    offset = (iota((LON_DEV, 128), 0) * PAIRS) & 127
    valid = ((lane - offset) & 127) < PAIRS
    return valid & (lane >= offset), valid & (lane < offset)


def forward_row(x, spread, twist, inner, pick):
    x = split(x)
    waves = []
    for member in range(2):
        rows = slice(256 * member, 256 * (member + 1))
        y = three(dot, (spread[0][rows], spread[1][rows]), x)
        re, im = y[:128], y[128:]
        rows = slice(128 * member, 128 * (member + 1))
        cos, sin = twist[0][rows], twist[1][rows]
        z = split(jnp.concatenate([re * cos + im * sin, im * cos - re * sin], axis=1))
        rows = slice(32 * member, 32 * (member + 1))
        waves.append(three(dot_nt, (inner[0][rows], inner[1][rows]), z).astype(bf16))
    stacked = jnp.concatenate(
        [waves[slot % 2][16 * (slot // 2) : 16 * (slot // 2 + 1)] for slot in range(4)], axis=1
    )
    values = dot(pick, stacked)
    straight, wrapped = lane_masks()
    message = None
    for slot in range(4):
        cols = slice(128 * slot, 128 * (slot + 1))
        own = jnp.where(
            straight, values[:LON_DEV, cols], jnp.where(wrapped, values[LON_DEV:, cols], 0.0)
        )
        own = pltpu.roll(own, 32 * slot, 1) if slot else own
        message = own if message is None else message + own
    return message


def column_products(rows, lon):
    r = iota((16 * GROUPS, 128), 0)
    target = lon * PAIRS + 32 * (((r >> 2) & 1) * 2 + ((r >> 3) & 1)) + 4 * (r >> 4) + (r & 3)
    order = (((iota((16 * GROUPS, 128), 1) - target) & 127) == 0).astype(f32).astype(bf16)
    q = dot_nt(order, rows.astype(bf16)).astype(bf16)
    source, lane = iota((64, 256), 0), iota((64, 256), 1)
    same = ((source >> 5) == (lane >> 7)) & ((source & 31) == (lane & 31))
    wide = dot(q, same.astype(f32).astype(bf16))
    own = ((iota(wide.shape, 1) >> 5) & 3) == (iota(wide.shape, 0) & 3)
    return jnp.where(own, wide, 0.0)


def slot_terms(shape, pair_first, slot_first):
    pair = pair_first + (iota(shape, 0) & 3)
    slot = slot_first + iota(shape, 1)
    upper = slot >= MT - pair
    odd = (jnp.where(upper, slot + pair, slot) & 1) == 1
    return pair, slot, upper, odd


def partial_solve(sums, pair_first, slot_first):
    shape = (8, sums.shape[1])
    pair, slot, upper, odd = slot_terms(shape, pair_first, slot_first)
    degree = jnp.where(upper, slot - 1, pair + slot)
    eigen = degree.astype(f32) * (degree + 1).astype(f32) / float(MT * MT)
    fields = []
    for field in range(3):
        block = [
            [sums[((par * 3 + field) * 2 + mem) * 8 :][:8] for mem in range(2)] for par in range(2)
        ]
        fields.append(
            jnp.where(
                upper,
                jnp.where(odd, block[1][1], block[0][1]),
                jnp.where(odd, block[1][0], block[0][0]),
            )
        )
    div_rhs = fields[1] - gravity_step * eigen * fields[2]
    height_spec = (fields[0] - time_step * div_rhs) / (1.0 + coupling * eigen)
    return height_spec, div_rhs + gravity_step * eigen * height_spec


def inverse_rows(solved, pair_first, slot_first):
    base = solved.astype(f32)
    _, _, upper, odd = slot_terms(base.shape, pair_first, slot_first)
    low, high = jnp.where(upper, 0.0, base), jnp.where(upper, base, 0.0)
    return jnp.concatenate(
        [low, high, jnp.where(odd, -low, low), jnp.where(odd, -high, high)], axis=0
    ).astype(bf16)


def own_pair(products):
    lane = iota((HALF, 64), 1) & 3
    total = None
    for pair in range(GROUP):
        term = jnp.where(lane == pair, products[HALF * pair : HALF * (pair + 1)], 0.0)
        total = term if total is None else total + term
    return total


def lane_order(lon, group):
    r, c = iota((64, 512), 0), iota((64, 512), 1)
    slot = ((r >> 2) & 1) * 2 + ((r >> 4) & 1)
    target = lon * PAIRS + 32 * slot + 4 * group + (r & 3)
    same = ((r >> 5) == (c >> 8)) & (((r >> 3) & 1) == ((c >> 7) & 1))
    return (same & (((c - target) & 127) == 0)).astype(f32).astype(bf16)


def inverse_row(c, spread_t, twist, back):
    straight, wrapped = lane_masks()
    mean = (iota((LON_DEV, 128), 0) == 0) & (iota((LON_DEV, 128), 1) == 0)
    total = None
    for member in range(2):
        stack = []
        for part in range(2):
            slot = part * 2 + member
            x = pltpu.roll(c, 128 - 32 * slot, 1) if slot else c
            if member == 0:
                x = jnp.where(mean, 0.5 * x, x)
            stack += [jnp.where(straight, x, 0.0), jnp.where(wrapped, x, 0.0)]
        x = split(jnp.concatenate(stack, axis=0).T)
        rows = slice(256 * member, 256 * (member + 1))
        b = three(dot, x, (back[0][rows], back[1][rows]))
        re, im = b[:, :256], b[:, 256:]
        rows = slice(128 * member, 128 * (member + 1))
        cos, sin = twist[0][rows], twist[1][rows]
        z = split(jnp.concatenate([re * cos - im * sin, re * sin + im * cos], axis=0))
        cols = slice(256 * member, 256 * (member + 1))
        term = three(dot, (spread_t[0][:, cols], spread_t[1][:, cols]), z)
        total = term if total is None else total + term
    return total


def kernel(
    height, divergence, depth, tide, weight_row,
    spread_h, spread_l, spread_th, spread_tl, twist_c, twist_s, inner_h, inner_l, pick, back_h, back_l,
    legendre,
    out_height, out_divergence,
    table, field_buf, tx1, rx1, tx2, rx2, tx4, rx4, tx5, rx5,
    columns, sums, sibling_sums, chip_tx, chip_rx, solved, message,
    table_sem, send_sem, recv_sem, own_sem, lat_send, lat_recv,
):
    lon, lat = lax.axis_index("lon"), lax.axis_index("lat")
    core = lax.rem(lat, 2)
    sibling = {"lat": lat + 1 - 2 * core}
    across = {"lat": lax.rem(lat + 2, 4)}
    mine = pl.multiple_of(core * PART, 128)
    theirs = pl.multiple_of(PART - core * PART, 128)

    def table_copy(g):
        rows = pl.ds(GROUP * g, GROUP)
        return pltpu.make_async_copy(legendre.at[rows], table.at[rows], table_sem.at[g])

    for g in range(GROUPS):
        table_copy(g).start()

    barrier = pltpu.get_barrier_semaphore()

    def greet(i, _):
        pl.semaphore_signal(barrier, 1, device_id={"lon": (lon + i) & (LON_DEV - 1)})
        return 0

    lax.fori_loop(1, LON_DEV, greet, 0)
    pl.semaphore_signal(barrier, 1, device_id=sibling)
    pl.semaphore_signal(barrier, 1, device_id=across)

    def exchange_start(phase, tx, rx):
        n = tx.shape[0] // LON_DEV
        own = pl.ds(lon * n, n)
        pltpu.make_async_copy(tx.at[own], rx.at[own], own_sem.at[phase]).start()

        def send(i, _):
            peer = (lon + i) & (LON_DEV - 1)
            pltpu.make_async_remote_copy(
                tx.at[pl.ds(peer * n, n)],
                rx.at[own],
                send_sem.at[phase],
                recv_sem.at[phase],
                device_id={"lon": peer},
            ).start()
            return 0

        lax.fori_loop(1, LON_DEV, send, 0)

    def exchange_wait(phase, tx, rx):
        n = tx.shape[0] // LON_DEV
        own = pl.ds(lon * n, n)
        rest = pl.ds(0, (LON_DEV - 1) * n)
        pltpu.make_async_copy(tx.at[own], rx.at[own], own_sem.at[phase]).wait()
        pltpu.make_async_copy(rx.at[rest], rx.at[rest], recv_sem.at[phase]).wait()
        pltpu.make_async_copy(tx.at[rest], tx.at[rest], send_sem.at[phase]).wait()

    weight = jnp.sum(
        jnp.where(
            iota((HALF, HALF), 0) == iota((HALF, HALF), 1),
            jnp.broadcast_to(weight_row[...], (HALF, HALF)),
            0.0,
        ),
        axis=1,
        keepdims=True,
    ) * (math.sqrt(NLON / NLAT) / MT / NLON)
    field_buf[...] = jnp.zeros_like(field_buf)
    fields = forcing_fields(height[...], divergence[...], depth[...], tide[...])
    for f in range(3):
        even, odd = fold(fields[f], weight)
        field_buf[0:HALF, 0:SPAN] = even
        field_buf[HALF:, 0:SPAN] = odd
        for h in range(2):
            tx1[pl.ds(2 * f + h, LON_DEV, stride=6), :] = field_buf[:, 128 * h : 128 * (h + 1)]

    pl.semaphore_wait(barrier, LON_DEV + 1)
    exchange_start(0, tx1, rx1)
    exchange_wait(0, tx1, rx1)

    spread = (spread_h, spread_l)
    twist = (twist_c, twist_s)
    inner = (inner_h, inner_l)
    for f in range(3):
        x = jnp.concatenate([rx1[pl.ds(2 * f + h, LON_DEV, stride=6), :] for h in range(2)], axis=1)
        tx2[pl.ds(f, LON_DEV, stride=3), :] = forward_row(x, spread, twist, inner, pick[...])
    exchange_start(1, tx2, rx2)
    exchange_wait(1, tx2, rx2)

    for f in range(3):
        wide = column_products(rx2[pl.ds(f, LON_DEV, stride=3), :], lon).astype(bf16)
        for g in range(GROUPS):
            for par in range(2):
                columns[g, 16 * (par * 3 + f) : 16 * (par * 3 + f + 1), :] = wide[
                    16 * g : 16 * (g + 1), 128 * par : 128 * (par + 1)
                ]

    def table_tail(g):
        last = table[pl.ds(GROUP * g, GROUP), :, SLOTS - 1 : SLOTS].reshape(128, 1).astype(f32)
        return jnp.where(iota((128, 128), 1) == 0, jnp.broadcast_to(last, (128, 128)), 0.0).astype(
            bf16
        )

    def table_tile(g, t):
        return table[pl.ds(GROUP * g, GROUP), :, TILE * t : TILE * (t + 1)].reshape(128, TILE)

    def tiles(g):
        for t in range(TILES):
            yield TILE * t, TILE, table_tile(g, t)
        yield TILE * TILES, 128, table_tail(g)

    def sibling_copy(g):
        return pltpu.make_async_remote_copy(
            sums.at[g, :, pl.ds(theirs, PART)],
            sibling_sums.at[g],
            lat_send.at[0, g],
            lat_recv.at[0, g],
            device_id=sibling,
        )

    def across_copy(g):
        return pltpu.make_async_remote_copy(
            chip_tx.at[g], chip_rx.at[g], lat_send.at[1, g], lat_recv.at[1, g], device_id=across
        )

    def share_copy(g):
        return pltpu.make_async_remote_copy(
            solved.at[g, :, pl.ds(mine, PART)],
            solved.at[g, :, pl.ds(mine, PART)],
            lat_send.at[2, g],
            lat_recv.at[2, g],
            device_id=sibling,
        )

    def forward_group(g):
        table_copy(g).wait()
        pair_first = lon * PAIRS + GROUP * g
        for first, width, rhs in tiles(g):
            both = partial_solve(dot(columns[g], rhs), pair_first, first)
            sums[g, 0:8, first : first + width] = both[0]
            sums[g, 8:16, first : first + width] = both[1]
        sums[g, :, WIDE - 128 : WIDE] = jnp.zeros((16, 128), f32)
        sibling_copy(g).start()

    def sibling_sum(g):
        sibling_copy(g).wait()
        total = sums[g, :, pl.ds(mine, PART)] + sibling_sums[g]
        sibling_sums[g] = total
        chip_tx[g] = total.astype(bf16)
        across_copy(g).start()

    def across_sum(g):
        across_copy(g).wait()
        total = sibling_sums[g] + chip_rx[g].astype(f32)
        solved[g, :, pl.ds(mine, PART)] = total.astype(bf16)
        share_copy(g).start()

    def inverse_group(g):
        share_copy(g).wait()
        pair_first = lon * PAIRS + GROUP * g
        total = None
        for first, width, rhs in tiles(g):
            rows = inverse_rows(solved[g, :, first : first + width], pair_first, first)
            term = dot_nt(rhs, rows)
            total = term if total is None else total + term
        high, low = split(own_pair(total))
        order = lane_order(lon, g)
        message[...] += dot(high, order) + dot(low, order)

    def forward_step(t, _):
        forward_group(t)

        @pl.when(t > 0)
        def _():
            sibling_sum(t - 1)

        return 0

    lax.fori_loop(0, GROUPS, forward_step, 0)
    sibling_sum(GROUPS - 1)

    message[...] = jnp.zeros_like(message)
    across_sum(0)

    def inverse_step(t, _):
        @pl.when(t + 1 < GROUPS)
        def _():
            across_sum(t + 1)

        inverse_group(t)
        return 0

    lax.fori_loop(0, GROUPS, inverse_step, 0)

    for field in range(2):
        for side in range(2):
            tx4[pl.ds(2 * HALF * side + field, HALF, stride=2), :] = message[
                :, 128 * (2 * side + field) : 128 * (2 * side + field + 1)
            ]
    exchange_start(2, tx4, rx4)
    exchange_wait(2, tx4, rx4)

    spread_t = (spread_th, spread_tl)
    back = (back_h, back_l)
    for field in range(2):
        grid = inverse_row(rx4[pl.ds(field, LON_DEV, stride=2), :], spread_t, twist, back)
        for h in range(2):
            tx5[pl.ds(2 * field + h, LON_DEV, stride=4), :] = grid[:, 128 * h : 128 * (h + 1)]
    exchange_start(3, tx5, rx5)
    exchange_wait(3, tx5, rx5)
    for field, out in enumerate((out_height, out_divergence)):
        out[:, 0:128] = rx5[pl.ds(2 * field, LON_DEV, stride=4), :]
        out[:, 128:SPAN] = rx5[pl.ds(2 * field + 1, LON_DEV, stride=4), :][:, : SPAN - 128]


def per_device(height, divergence, depth, tide, gauss_weight, legendre):
    consts = [jnp.asarray(t) for t in tables()]
    vmem = pl.BlockSpec(memory_space=pltpu.VMEM)
    grid_shape = jax.ShapeDtypeStruct(height.shape, f32)

    def pair(rows, dtype=f32):
        return [pltpu.VMEM((LON_DEV * rows, 128), dtype)] * 2

    return pl.pallas_call(
        kernel,
        out_shape=(grid_shape, grid_shape),
        in_specs=[vmem] * (5 + len(consts)) + [pl.BlockSpec(memory_space=pl.ANY)],
        out_specs=(vmem, vmem),
        scratch_shapes=[
            pltpu.VMEM((PAIRS, HALF, SLOTS), bf16),
            pltpu.VMEM((2 * HALF, 256), f32),
            *pair(6),
            *pair(3),
            *pair(2),
            *pair(4),
            pltpu.VMEM((GROUPS, 96, 128), bf16),
            pltpu.VMEM((GROUPS, 16, WIDE), f32),
            pltpu.VMEM((GROUPS, 16, PART), f32),
            pltpu.VMEM((GROUPS, 16, PART), bf16),
            pltpu.VMEM((GROUPS, 16, PART), bf16),
            pltpu.VMEM((GROUPS, 16, WIDE), bf16),
            pltpu.VMEM((HALF, 512), f32),
            pltpu.SemaphoreType.DMA((GROUPS,)),
            pltpu.SemaphoreType.DMA((4,)),
            pltpu.SemaphoreType.DMA((4,)),
            pltpu.SemaphoreType.DMA((4,)),
            pltpu.SemaphoreType.DMA((3, GROUPS)),
            pltpu.SemaphoreType.DMA((3, GROUPS)),
        ],
        compiler_params=pltpu.CompilerParams(
            collective_id=0, has_side_effects=True, vmem_limit_bytes=48 << 20
        ),
    )(height, divergence, depth, tide, gauss_weight.reshape(1, HALF), *consts, legendre)


def solution(mesh):
    in_specs = (
        P("lat", "lon"),
        P("lat", "lon"),
        P("lat", "lon"),
        P("lat", "lon"),
        P("lat"),
        P("lon", "lat", None),
    )
    out_specs = (P("lat", "lon"), P("lat", "lon"))
    return jax.shard_map(
        per_device, mesh=mesh, in_specs=in_specs, out_specs=out_specs, check_vma=False
    )
```

```python
import math

import jax
import jax.numpy as jnp
import ml_dtypes
import numpy as np
from jax import lax
from jax.experimental import pallas as pl
from jax.experimental.pallas import tpu as pltpu
from jax.sharding import PartitionSpec as P

time_step = 0.5
drag_step = 0.1
coupling = 2.0
gravity_step = 4.0

f32, bf16 = jnp.float32, jnp.bfloat16

LON_DEV = 64
SPAN = 250
NLON = LON_DEV * SPAN
PAIRS = 28
MT = 2 * PAIRS * LON_DEV
SLOTS = MT + 1
HALF = 32
NLAT = 256
GROUP = 4
GROUPS = PAIRS // GROUP
TILE = 512
TILES = (SLOTS - 1) // TILE


def two_terms(table):
    high = table.astype(ml_dtypes.bfloat16)
    low = (table - high.astype(np.float64)).astype(ml_dtypes.bfloat16)
    return high, low


def tables():
    v, tau, s, j = np.arange(128), np.arange(16), np.arange(LON_DEV), np.arange(256)
    real = (j < SPAN).astype(np.float64)
    psi = 2 * np.pi * (np.outer(s, s) % LON_DEV) / LON_DEV
    spread = np.concatenate([np.cos(psi), -np.sin(psi)])
    first = np.stack([v, MT - v])
    theta = 2 * np.pi * ((first[:, :, None] * j) % NLON) / NLON
    twist_cos = (np.cos(theta) * real).reshape(256, 256).astype(np.float32)
    twist_sin = (np.sin(theta) * real).reshape(256, 256).astype(np.float32)

    def over_j(row, scale):
        phi = 2 * np.pi * ((128 * row[..., None] * j) % NLON) / NLON
        return scale * np.cos(phi) * real, scale * np.sin(phi) * real

    cos, sin = over_j(np.stack([tau, -tau]), 1)
    inner = np.concatenate(
        [np.concatenate([cos, sin], axis=2), np.concatenate([-sin, cos], axis=2)], axis=1
    ).reshape(64, 512)
    row = np.stack([(PAIRS * s) // 128, (PAIRS * s + 1) // 128])
    row = np.concatenate([row, row + 1], axis=1)
    pick = (row[..., None] == tau).reshape(256, 16)
    cos, sin = over_j(row * np.array([[1], [-1]]), 2)
    back = np.concatenate(
        [np.concatenate([cos, sin], axis=2), np.concatenate([-sin, cos], axis=2)], axis=1
    ).reshape(512, 512)
    return (
        *two_terms(spread),
        *two_terms(np.ascontiguousarray(spread.T)),
        twist_cos,
        twist_sin,
        *two_terms(inner),
        pick.astype(ml_dtypes.bfloat16),
        *two_terms(back),
    )


def iota(shape, dim):
    return lax.broadcasted_iota(jnp.int32, shape, dim)


def dot(a, b):
    return lax.dot_general(a, b, (((1,), (0,)), ((), ())), preferred_element_type=f32)


def dot_nt(a, b):
    return lax.dot_general(a, b, (((1,), (1,)), ((), ())), preferred_element_type=f32)


def split(x):
    high = x.astype(bf16)
    return high, (x - high.astype(f32)).astype(bf16)


def three(product, a, b):
    return product(a[0], b[0]) + (product(a[0], b[1]) + product(a[1], b[0]))


def forcing_fields(height, divergence, depth, tide):
    return (
        height - time_step * (depth - 1.0) * divergence,
        divergence * (1.0 - drag_step / depth),
        tide,
    )


def fold(field, weight):
    north, south = field[:HALF], field[HALF:]
    return (north + south) * weight, (north - south) * weight


def lane_masks(member):
    lane = iota((LON_DEV, 128), 1)
    offset = (iota((LON_DEV, 128), 0) * PAIRS + member) & 127
    valid = ((lane - offset) & 127) < PAIRS
    return valid & (lane >= offset), valid & (lane < offset)


def twice(x):
    return jnp.concatenate([x, x], axis=0)


def forward_row(x, spread, twist, inner, pick):
    y = three(dot, spread, split(x))
    re, im = twice(y[:LON_DEV]), twice(y[LON_DEV:])
    message = None
    for member in range(2):
        rows = slice(128 * member, 128 * (member + 1))
        cos, sin = twist[0][rows], twist[1][rows]
        if member == 0:
            z = [re * cos + im * sin, im * cos - re * sin]
        else:
            z = [re * cos - im * sin, -(im * cos + re * sin)]
        z = split(jnp.concatenate(z, axis=1))
        cols = slice(32 * member, 32 * (member + 1))
        waves = three(dot_nt, (inner[0][cols], inner[1][cols]), z).astype(bf16)
        values = dot(pick[rows], jnp.concatenate([waves[:16], waves[16:]], axis=1))
        straight, wrapped = lane_masks(member)
        for part in range(2):
            slot = part * 2 + member
            cols = slice(128 * part, 128 * (part + 1))
            own = jnp.where(
                straight, values[:LON_DEV, cols], jnp.where(wrapped, values[LON_DEV:, cols], 0.0)
            )
            own = pltpu.roll(own, 32 * slot, 1) if slot else own
            message = own if message is None else message + own
    return message


def column_products(rows, lon):
    r = iota((16 * GROUPS, 128), 0)
    member, part = (r >> 3) & 1, (r >> 2) & 1
    target = lon * PAIRS + 64 * part + 33 * member + 4 * (r >> 4) + (r & 3)
    order = (((iota((16 * GROUPS, 128), 1) - target) & 127) == 0).astype(f32).astype(bf16)
    q = dot_nt(order, rows.astype(bf16)).astype(bf16)
    source, lane = iota((64, 256), 0), iota((64, 256), 1)
    same = ((source >> 5) == (lane >> 7)) & ((source & 31) == (lane & 31))
    wide = dot(q, same.astype(f32).astype(bf16))
    own = ((iota(wide.shape, 1) >> 5) & 3) == (iota(wide.shape, 0) & 3)
    return jnp.where(own, wide, 0.0)


def slot_terms(shape, pair_first, slot_first):
    pair = pair_first + (iota(shape, 0) & 3)
    slot = slot_first + iota(shape, 1)
    upper = slot >= MT - pair
    odd = (jnp.where(upper, slot + pair, slot) & 1) == 1
    return pair, slot, upper, odd


def partial_solve(sums, pair_first, slot_first):
    shape = (8, sums.shape[1])
    pair, slot, upper, odd = slot_terms(shape, pair_first, slot_first)
    degree = jnp.where(upper, slot - 1, pair + slot)
    eigen = degree.astype(f32) * (degree + 1).astype(f32) / float(MT * MT)
    fields = []
    for field in range(3):
        block = [
            [sums[((par * 3 + field) * 2 + mem) * 8 :][:8] for mem in range(2)] for par in range(2)
        ]
        fields.append(
            jnp.where(
                upper,
                jnp.where(odd, block[1][1], block[0][1]),
                jnp.where(odd, block[1][0], block[0][0]),
            )
        )
    div_rhs = fields[1] - gravity_step * eigen * fields[2]
    height_spec = (fields[0] - time_step * div_rhs) / (1.0 + coupling * eigen)
    return height_spec, div_rhs + gravity_step * eigen * height_spec


def inverse_rows(solved, pair_first, slot_first):
    _, _, upper, odd = slot_terms(solved[0].shape, pair_first, slot_first)
    base = [x.astype(f32) for x in solved]
    rows = [jnp.where(upper, 0.0, x) for x in base] + [jnp.where(upper, x, 0.0) for x in base]
    rows += [jnp.where(odd, -x, x) for x in rows]
    return jnp.concatenate(rows, axis=0).astype(bf16)


def own_pair(products):
    lane = iota((HALF, 64), 1) & 3
    total = None
    for pair in range(GROUP):
        term = jnp.where(lane == pair, products[HALF * pair : HALF * (pair + 1)], 0.0)
        total = term if total is None else total + term
    return total


def lane_order(lon, group):
    r, c = iota((64, 512), 0), iota((64, 512), 1)
    member, part = (r >> 4) & 1, (r >> 2) & 1
    target = lon * PAIRS + 64 * part + 33 * member + 4 * group + (r & 3)
    same = ((r >> 5) == (c >> 8)) & (((r >> 3) & 1) == ((c >> 7) & 1))
    return (same & (((c - target) & 127) == 0)).astype(f32).astype(bf16)


def inverse_row(c, spread_t, twist, back):
    mean = (iota((LON_DEV, 128), 0) == 0) & (iota((LON_DEV, 128), 1) == 0)
    total = None
    for member in range(2):
        straight, wrapped = lane_masks(member)
        stack = []
        for part in range(2):
            slot = part * 2 + member
            x = pltpu.roll(c, 128 - 32 * slot, 1) if slot else c
            if member == 0:
                x = jnp.where(mean, 0.5 * x, x)
            stack += [jnp.where(straight, x, 0.0), jnp.where(wrapped, x, 0.0)]
        x = split(jnp.concatenate(stack, axis=0).T)
        rows = slice(256 * member, 256 * (member + 1))
        b = three(dot, x, (back[0][rows], back[1][rows]))
        re, im = b[:, :256], b[:, 256:]
        rows = slice(128 * member, 128 * (member + 1))
        cos, sin = twist[0][rows], twist[1][rows]
        z = [re * cos - im * sin, re * sin + im * cos]
        z = [part[:LON_DEV] + part[LON_DEV:] for part in z]
        total = z if total is None else [total[0] + z[0], total[1] - z[1]]
    return three(dot, spread_t, split(jnp.concatenate(total, axis=0)))


CONSTS = 11


def kernel(*refs):
    grid_in, refs = refs[:5], refs[5:]
    consts_in, refs = refs[:CONSTS], refs[CONSTS:]
    legendre, out_height, out_divergence, *refs = refs
    grid, refs = refs[:5], refs[5:]
    consts, refs = refs[:CONSTS], refs[CONSTS:]
    table, field_buf, tx1, rx1, tx2, rx2, tx4, rx4, tx5, rx5, *refs = refs
    columns, sums, sibling_sums, chip_tx, chip_rx, solved, message, *refs = refs
    in_sem, table_sem, send_sem, recv_sem, own_sem, lat_send, lat_recv = refs
    lon, lat = lax.axis_index("lon"), lax.axis_index("lat")
    core = lax.rem(lat, 2)
    sibling = {"lat": lat + 1 - 2 * core}
    across = {"lat": lax.rem(lat + 2, 4)}

    def peers(visit):
        x, z, y = lon >> 5, (lon >> 2) & 7, lon & 3
        for step in (4, 3, 5, 2, 6, 1, 7, 0):
            far = ((z + step) & 7) << 2

            def one(i, _):
                order = i >> 1
                turn = jnp.where(order == 0, 2, jnp.where(order == 1, 1, jnp.where(order == 2, 3, 0)))
                visit(((x ^ (1 - (i & 1))) << 5) | far | ((y + turn) & 3))
                return 0

            lax.fori_loop(0, 8 if step else 7, one, 0)

    def table_copy(g):
        rows = pl.ds(GROUP * g, GROUP)
        return pltpu.make_async_copy(legendre.at[rows], table.at[rows], table_sem.at[g])

    grid_copies = [
        pltpu.make_async_copy(a, b, in_sem.at[n]) for n, (a, b) in enumerate(zip(grid_in, grid))
    ]
    const_copies = [
        pltpu.make_async_copy(a, b, in_sem.at[5 + n])
        for n, (a, b) in enumerate(zip(consts_in, consts))
    ]
    for copy in grid_copies:
        copy.start()
    barrier = pltpu.get_barrier_semaphore()
    peers(lambda peer: pl.semaphore_signal(barrier, 1, device_id={"lon": peer}))
    pl.semaphore_signal(barrier, 1, device_id=sibling)
    pl.semaphore_signal(barrier, 1, device_id=across)
    for copy in const_copies:
        copy.start()
    for g in range(GROUPS):
        table_copy(g).start()

    def exchange_start(phase, tx, rx):
        n = tx.shape[0] // LON_DEV
        own = pl.ds(lon * n, n)
        peers(
            lambda peer: pltpu.make_async_remote_copy(
                tx.at[pl.ds(peer * n, n)],
                rx.at[own],
                send_sem.at[phase],
                recv_sem.at[phase],
                device_id={"lon": peer},
            ).start()
        )
        pltpu.make_async_copy(tx.at[own], rx.at[own], own_sem.at[phase]).start()

    def exchange_wait(phase, tx, rx):
        n = tx.shape[0] // LON_DEV
        own = pl.ds(lon * n, n)
        rest = pl.ds(0, (LON_DEV - 1) * n)
        pltpu.make_async_copy(tx.at[own], rx.at[own], own_sem.at[phase]).wait()
        pltpu.make_async_copy(rx.at[rest], rx.at[rest], recv_sem.at[phase]).wait()

    def exchange_sent(phase, tx):
        rest = pl.ds(0, (LON_DEV - 1) * (tx.shape[0] // LON_DEV))
        pltpu.make_async_copy(tx.at[rest], tx.at[rest], send_sem.at[phase]).wait()

    for copy in grid_copies:
        copy.wait()
    height, divergence, depth, tide, weight_row = grid
    weight = jnp.sum(
        jnp.where(
            iota((HALF, HALF), 0) == iota((HALF, HALF), 1),
            jnp.broadcast_to(weight_row[...], (HALF, HALF)),
            0.0,
        ),
        axis=1,
        keepdims=True,
    ) * (math.sqrt(NLON / NLAT) / MT / NLON)
    field_buf[...] = jnp.zeros_like(field_buf)
    fields = forcing_fields(height[...], divergence[...], depth[...], tide[...])
    for f in range(3):
        even, odd = fold(fields[f], weight)
        field_buf[0:HALF, 0:SPAN] = even
        field_buf[HALF:, 0:SPAN] = odd
        for h in range(2):
            tx1[pl.ds(2 * f + h, LON_DEV, stride=6), :] = field_buf[:, 128 * h : 128 * (h + 1)]

    pl.semaphore_wait(barrier, LON_DEV + 1)
    exchange_start(0, tx1, rx1)
    for copy in const_copies:
        copy.wait()
    spread, spread_t, twist, inner, back = (consts[n : n + 2] for n in (0, 2, 4, 6, 9))
    spread, spread_t = [r[...] for r in spread], [r[...] for r in spread_t]
    pick = consts[8]
    exchange_wait(0, tx1, rx1)

    for f in range(3):
        x = jnp.concatenate([rx1[pl.ds(2 * f + h, LON_DEV, stride=6), :] for h in range(2)], axis=1)
        tx2[pl.ds(f, LON_DEV, stride=3), :] = forward_row(x, spread, twist, inner, pick)
    exchange_start(1, tx2, rx2)
    exchange_wait(1, tx2, rx2)

    for f in range(3):
        wide = column_products(rx2[pl.ds(f, LON_DEV, stride=3), :], lon).astype(bf16)
        for g in range(GROUPS):
            for par in range(2):
                columns[g, 16 * (par * 3 + f) : 16 * (par * 3 + f + 1), :] = wide[
                    16 * g : 16 * (g + 1), 128 * par : 128 * (par + 1)
                ]

    def table_tail(g):
        last = table[pl.ds(GROUP * g, GROUP), :, SLOTS - 1 : SLOTS].reshape(128, 1).astype(f32)
        return jnp.where(iota((128, 128), 1) == 0, jnp.broadcast_to(last, (128, 128)), 0.0).astype(
            bf16
        )

    def table_tile(g, t):
        return table[pl.ds(GROUP * g, GROUP), :, TILE * t : TILE * (t + 1)].reshape(128, TILE)

    def tiles(g):
        for t in range(TILES):
            yield TILE * t, TILE, table_tile(g, t)
        yield TILE * TILES, 128, table_tail(g)

    def sibling_copy(g):
        return pltpu.make_async_remote_copy(
            sums.at[g, 1 - core],
            sibling_sums.at[g],
            lat_send.at[0, g],
            lat_recv.at[0, g],
            device_id=sibling,
        )

    def across_copy(g):
        return pltpu.make_async_remote_copy(
            chip_tx.at[g], chip_rx.at[g], lat_send.at[1, g], lat_recv.at[1, g], device_id=across
        )

    def share_copy(g):
        return pltpu.make_async_remote_copy(
            solved.at[g, core],
            solved.at[g, core],
            lat_send.at[2, g],
            lat_recv.at[2, g],
            device_id=sibling,
        )

    def forward_group(g):
        table_copy(g).wait()
        pair_first = lon * PAIRS + GROUP * g
        for first, width, rhs in tiles(g):
            both = partial_solve(dot(columns[g], rhs), pair_first, first)
            for field in range(2):
                sums[g, field, :, first : first + width] = both[field]
        sibling_copy(g).start()

    def sibling_sum(g):
        sibling_copy(g).wait_recv()
        total = sums[g, core] + sibling_sums[g]
        chip_tx[g] = total.astype(bf16)
        across_copy(g).start()
        sibling_sums[g] = total

    def across_sum(g):
        across_copy(g).wait_recv()
        total = sibling_sums[g] + chip_rx[g].astype(f32)
        solved[g, core] = total.astype(bf16)
        share_copy(g).start()

    def inverse_group(g):
        share_copy(g).wait_recv()
        pair_first = lon * PAIRS + GROUP * g
        total = None
        for first, width, rhs in tiles(g):
            both = [solved[g, field, :, first : first + width] for field in range(2)]
            term = dot_nt(rhs, inverse_rows(both, pair_first, first))
            total = term if total is None else total + term
        high, low = split(own_pair(total))
        order = lane_order(lon, g)
        message[...] += dot(high, order) + dot(low, order)

    def forward_step(t, _):
        forward_group(t)

        @pl.when(t > 0)
        def _():
            sibling_sum(t - 1)

        return 0

    lax.fori_loop(0, GROUPS, forward_step, 0)
    sibling_sum(GROUPS - 1)

    message[...] = jnp.zeros_like(message)
    across_sum(0)

    def inverse_step(t, _):
        @pl.when(t + 1 < GROUPS)
        def _():
            across_sum(t + 1)

        inverse_group(t)
        return 0

    lax.fori_loop(0, GROUPS, inverse_step, 0)

    for field in range(2):
        for side in range(2):
            tx4[pl.ds(2 * HALF * side + field, HALF, stride=2), :] = message[
                :, 128 * (2 * side + field) : 128 * (2 * side + field + 1)
            ]
    exchange_start(2, tx4, rx4)
    exchange_wait(2, tx4, rx4)

    for field in range(2):
        grid = inverse_row(rx4[pl.ds(field, LON_DEV, stride=2), :], spread_t, twist, back)
        for h in range(2):
            tx5[pl.ds(2 * field + h, LON_DEV, stride=4), :] = grid[:, 128 * h : 128 * (h + 1)]
    exchange_start(3, tx5, rx5)
    exchange_wait(3, tx5, rx5)
    for field, out in enumerate((out_height, out_divergence)):
        out[:, 0:128] = rx5[pl.ds(2 * field, LON_DEV, stride=4), :]
        out[:, 128:SPAN] = rx5[pl.ds(2 * field + 1, LON_DEV, stride=4), :][:, : SPAN - 128]

    for phase, tx in enumerate((tx1, tx2, tx4, tx5)):
        exchange_sent(phase, tx)
    for g in range(GROUPS):
        for copy in (sibling_copy, across_copy, share_copy):
            copy(g).wait_send()


def per_device(height, divergence, depth, tide, gauss_weight, legendre):
    consts = [jnp.asarray(t) for t in tables()]
    grid = (height, divergence, depth, tide, gauss_weight.reshape(1, HALF))
    vmem, hbm = pl.BlockSpec(memory_space=pltpu.VMEM), pl.BlockSpec(memory_space=pltpu.HBM)
    grid_shape = jax.ShapeDtypeStruct(height.shape, f32)

    def pair(rows):
        return [pltpu.VMEM((LON_DEV * rows, 128), f32)] * 2

    wide = 128 * pl.cdiv(SLOTS, 128)
    return pl.pallas_call(
        kernel,
        out_shape=(grid_shape, grid_shape),
        in_specs=[hbm] * (len(grid) + len(consts) + 1),
        out_specs=(vmem, vmem),
        scratch_shapes=[
            *[pltpu.VMEM(x.shape, x.dtype) for x in (*grid, *consts)],
            pltpu.VMEM((PAIRS, HALF, SLOTS), bf16),
            pltpu.VMEM((2 * HALF, 256), f32),
            *pair(6),
            *pair(3),
            *pair(2),
            *pair(4),
            pltpu.VMEM((GROUPS, 96, 128), bf16),
            pltpu.VMEM((GROUPS, 2, 8, wide), f32),
            pltpu.VMEM((GROUPS, 8, wide), f32),
            pltpu.VMEM((GROUPS, 8, wide), bf16),
            pltpu.VMEM((GROUPS, 8, wide), bf16),
            pltpu.VMEM((GROUPS, 2, 8, wide), bf16),
            pltpu.VMEM((HALF, 512), f32),
            pltpu.SemaphoreType.DMA((5 + CONSTS,)),
            pltpu.SemaphoreType.DMA((GROUPS,)),
            pltpu.SemaphoreType.DMA((4,)),
            pltpu.SemaphoreType.DMA((4,)),
            pltpu.SemaphoreType.DMA((4,)),
            pltpu.SemaphoreType.DMA((3, GROUPS)),
            pltpu.SemaphoreType.DMA((3, GROUPS)),
        ],
        compiler_params=pltpu.CompilerParams(
            collective_id=0, has_side_effects=True, vmem_limit_bytes=48 << 20
        ),
    )(*grid, *consts, legendre)


def solution(mesh):
    in_specs = (
        P("lat", "lon"),
        P("lat", "lon"),
        P("lat", "lon"),
        P("lat", "lon"),
        P("lat"),
        P("lon", "lat", None),
    )
    out_specs = (P("lat", "lon"), P("lat", "lon"))
    return jax.shard_map(
        per_device, mesh=mesh, in_specs=in_specs, out_specs=out_specs, check_vma=False
    )
```

```python
import math

import jax
import jax.numpy as jnp
import ml_dtypes
import numpy as np
from jax import lax
from jax.experimental import pallas as pl
from jax.experimental.pallas import tpu as pltpu
from jax.sharding import PartitionSpec as P

time_step = 0.5
drag_step = 0.1
coupling = 2.0
gravity_step = 4.0

f32, bf16 = jnp.float32, jnp.bfloat16

LON_DEV = 64
SPAN = 250
NLON = LON_DEV * SPAN
PAIRS = 28
MT = 2 * PAIRS * LON_DEV
SLOTS = MT + 1
HALF = 32
NLAT = 256
GROUP = 4
GROUPS = PAIRS // GROUP
TILE = 512
TILES = (SLOTS - 1) // TILE


def two_terms(table):
    high = table.astype(ml_dtypes.bfloat16)
    low = (table - high.astype(np.float64)).astype(ml_dtypes.bfloat16)
    return high, low


def tables():
    v, tau, s, j = np.arange(128), np.arange(16), np.arange(LON_DEV), np.arange(256)
    real = (j < SPAN).astype(np.float64)
    psi = 2 * np.pi * (np.outer(s, s) % LON_DEV) / LON_DEV
    spread = np.concatenate([np.cos(psi), -np.sin(psi)])
    first = np.stack([v, MT - v])
    theta = 2 * np.pi * ((first[:, :, None] * j) % NLON) / NLON
    twist_cos = (np.cos(theta) * real).reshape(256, 256).astype(np.float32)
    twist_sin = (np.sin(theta) * real).reshape(256, 256).astype(np.float32)

    def over_j(row, scale):
        phi = 2 * np.pi * ((128 * row[..., None] * j) % NLON) / NLON
        return scale * np.cos(phi) * real, scale * np.sin(phi) * real

    cos, sin = over_j(np.stack([tau, -tau]), 1)
    inner = np.concatenate(
        [np.concatenate([cos, sin], axis=2), np.concatenate([-sin, cos], axis=2)], axis=1
    ).reshape(64, 512)
    row = np.stack([(PAIRS * s) // 128, (PAIRS * s + 1) // 128])
    row = np.concatenate([row, row + 1], axis=1)
    pick = (row[..., None] == tau).reshape(256, 16)
    cos, sin = over_j(row * np.array([[1], [-1]]), 2)
    back = np.concatenate(
        [np.concatenate([cos, sin], axis=2), np.concatenate([-sin, cos], axis=2)], axis=1
    ).reshape(512, 512)
    return (
        *two_terms(spread),
        *two_terms(np.ascontiguousarray(spread.T)),
        twist_cos,
        twist_sin,
        *two_terms(inner),
        pick.astype(ml_dtypes.bfloat16),
        *two_terms(back),
    )


def iota(shape, dim):
    return lax.broadcasted_iota(jnp.int32, shape, dim)


def dot(a, b):
    return lax.dot_general(a, b, (((1,), (0,)), ((), ())), preferred_element_type=f32)


def dot_nt(a, b):
    return lax.dot_general(a, b, (((1,), (1,)), ((), ())), preferred_element_type=f32)


def split(x):
    high = x.astype(bf16)
    return high, (x - high.astype(f32)).astype(bf16)


def three(product, a, b):
    return product(a[0], b[0]) + (product(a[0], b[1]) + product(a[1], b[0]))


def forcing_fields(height, divergence, depth, tide):
    return (
        height - time_step * (depth - 1.0) * divergence,
        divergence * (1.0 - drag_step / depth),
        tide,
    )


def fold(field, weight):
    north, south = field[:HALF], field[HALF:]
    return (north + south) * weight, (north - south) * weight


def lane_masks(member):
    lane = iota((LON_DEV, 128), 1)
    offset = (iota((LON_DEV, 128), 0) * PAIRS + member) & 127
    valid = ((lane - offset) & 127) < PAIRS
    return valid & (lane >= offset), valid & (lane < offset)


def twice(x):
    return jnp.concatenate([x, x], axis=0)


def forward_row(x, spread, twist, inner, pick):
    y = three(dot, spread, split(x))
    re, im = twice(y[:LON_DEV]), twice(y[LON_DEV:])
    message = None
    for member in range(2):
        rows = slice(128 * member, 128 * (member + 1))
        cos, sin = twist[0][rows], twist[1][rows]
        if member == 0:
            z = [re * cos + im * sin, im * cos - re * sin]
        else:
            z = [re * cos - im * sin, -(im * cos + re * sin)]
        z = split(jnp.concatenate(z, axis=1))
        cols = slice(32 * member, 32 * (member + 1))
        waves = three(dot_nt, (inner[0][cols], inner[1][cols]), z).astype(bf16)
        values = dot(pick[rows], jnp.concatenate([waves[:16], waves[16:]], axis=1))
        straight, wrapped = lane_masks(member)
        for part in range(2):
            slot = part * 2 + member
            cols = slice(128 * part, 128 * (part + 1))
            own = jnp.where(
                straight, values[:LON_DEV, cols], jnp.where(wrapped, values[LON_DEV:, cols], 0.0)
            )
            own = pltpu.roll(own, 32 * slot, 1) if slot else own
            message = own if message is None else message + own
    return message


def column_products(rows, lon):
    r = iota((16 * GROUPS, 128), 0)
    member, part = (r >> 3) & 1, (r >> 2) & 1
    target = lon * PAIRS + 64 * part + 33 * member + 4 * (r >> 4) + (r & 3)
    order = (((iota((16 * GROUPS, 128), 1) - target) & 127) == 0).astype(f32).astype(bf16)
    q = dot_nt(order, rows.astype(bf16)).astype(bf16)
    source, lane = iota((64, 256), 0), iota((64, 256), 1)
    same = ((source >> 5) == (lane >> 7)) & ((source & 31) == (lane & 31))
    wide = dot(q, same.astype(f32).astype(bf16))
    own = ((iota(wide.shape, 1) >> 5) & 3) == (iota(wide.shape, 0) & 3)
    return jnp.where(own, wide, 0.0)


def slot_terms(shape, pair_first, slot_first):
    pair = pair_first + (iota(shape, 0) & 3)
    slot = slot_first + iota(shape, 1)
    upper = slot >= MT - pair
    odd = (jnp.where(upper, slot + pair, slot) & 1) == 1
    return pair, slot, upper, odd


def partial_solve(sums, pair_first, slot_first):
    shape = (8, sums.shape[1])
    pair, slot, upper, odd = slot_terms(shape, pair_first, slot_first)
    degree = jnp.where(upper, slot - 1, pair + slot)
    eigen = degree.astype(f32) * (degree + 1).astype(f32) / float(MT * MT)
    fields = []
    for field in range(3):
        block = [
            [sums[((par * 3 + field) * 2 + mem) * 8 :][:8] for mem in range(2)] for par in range(2)
        ]
        fields.append(
            jnp.where(
                upper,
                jnp.where(odd, block[1][1], block[0][1]),
                jnp.where(odd, block[1][0], block[0][0]),
            )
        )
    div_rhs = fields[1] - gravity_step * eigen * fields[2]
    height_spec = (fields[0] - time_step * div_rhs) / (1.0 + coupling * eigen)
    return height_spec, div_rhs + gravity_step * eigen * height_spec


def inverse_rows(solved, pair_first, slot_first):
    _, _, upper, odd = slot_terms(solved[0].shape, pair_first, slot_first)
    base = [x.astype(f32) for x in solved]
    rows = [jnp.where(upper, 0.0, x) for x in base] + [jnp.where(upper, x, 0.0) for x in base]
    rows += [jnp.where(odd, -x, x) for x in rows]
    return jnp.concatenate(rows, axis=0).astype(bf16)


def own_pair(products):
    lane = iota((HALF, 64), 1) & 3
    total = None
    for pair in range(GROUP):
        term = jnp.where(lane == pair, products[HALF * pair : HALF * (pair + 1)], 0.0)
        total = term if total is None else total + term
    return total


def lane_order(lon, group):
    r, c = iota((64, 512), 0), iota((64, 512), 1)
    member, part = (r >> 4) & 1, (r >> 2) & 1
    target = lon * PAIRS + 64 * part + 33 * member + 4 * group + (r & 3)
    same = ((r >> 5) == (c >> 8)) & (((r >> 3) & 1) == ((c >> 7) & 1))
    return (same & (((c - target) & 127) == 0)).astype(f32).astype(bf16)


def inverse_row(c, spread_t, twist, back):
    mean = (iota((LON_DEV, 128), 0) == 0) & (iota((LON_DEV, 128), 1) == 0)
    total = None
    for member in range(2):
        straight, wrapped = lane_masks(member)
        stack = []
        for part in range(2):
            slot = part * 2 + member
            x = pltpu.roll(c, 128 - 32 * slot, 1) if slot else c
            if member == 0:
                x = jnp.where(mean, 0.5 * x, x)
            stack += [jnp.where(straight, x, 0.0), jnp.where(wrapped, x, 0.0)]
        x = split(jnp.concatenate(stack, axis=0).T)
        rows = slice(256 * member, 256 * (member + 1))
        b = three(dot, x, (back[0][rows], back[1][rows]))
        re, im = b[:, :256], b[:, 256:]
        rows = slice(128 * member, 128 * (member + 1))
        cos, sin = twist[0][rows], twist[1][rows]
        z = [re * cos - im * sin, re * sin + im * cos]
        z = [part[:LON_DEV] + part[LON_DEV:] for part in z]
        total = z if total is None else [total[0] + z[0], total[1] - z[1]]
    return three(dot, spread_t, split(jnp.concatenate(total, axis=0)))


CONSTS = 11


def kernel(*refs):
    grid_in, refs = refs[:5], refs[5:]
    consts_in, refs = refs[:CONSTS], refs[CONSTS:]
    legendre, out_height, out_divergence, *refs = refs
    grid, refs = refs[:5], refs[5:]
    consts, refs = refs[:CONSTS], refs[CONSTS:]
    table, field_buf, tx1, rx1, tx2, rx2, tx4, rx4, tx5, rx5, *refs = refs
    columns, sums, sibling_sums, chip_tx, chip_rx, solved, message, *refs = refs
    in_sem, table_sem, send_sem, recv_sem, own_sem, lat_send, lat_recv = refs
    lon, lat = lax.axis_index("lon"), lax.axis_index("lat")
    core = lax.rem(lat, 2)
    sibling = {"lat": lat + 1 - 2 * core}
    across = {"lat": lax.rem(lat + 2, 4)}

    def peers(visit):
        x, z, y = lon >> 5, (lon >> 2) & 7, lon & 3
        for step in (4, 3, 5, 2, 6, 1, 7, 0):
            far = ((z + step) & 7) << 2

            def one(i, _):
                order = i >> 1
                turn = jnp.where(order == 0, 2, jnp.where(order == 1, 1, jnp.where(order == 2, 3, 0)))
                visit(((x ^ (1 - (i & 1))) << 5) | far | ((y + turn) & 3))
                return 0

            lax.fori_loop(0, 8 if step else 7, one, 0)

    def table_copy(g):
        rows = pl.ds(GROUP * g, GROUP)
        return pltpu.make_async_copy(legendre.at[rows], table.at[rows], table_sem.at[g])

    grid_copies = [
        pltpu.make_async_copy(a, b, in_sem.at[n]) for n, (a, b) in enumerate(zip(grid_in, grid))
    ]
    const_copies = [
        pltpu.make_async_copy(a, b, in_sem.at[5 + n])
        for n, (a, b) in enumerate(zip(consts_in, consts))
    ]
    for copy in grid_copies:
        copy.start()
    barrier = pltpu.get_barrier_semaphore()
    peers(lambda peer: pl.semaphore_signal(barrier, 1, device_id={"lon": peer}))
    pl.semaphore_signal(barrier, 1, device_id=sibling)
    pl.semaphore_signal(barrier, 1, device_id=across)
    for copy in const_copies:
        copy.start()
    for g in range(GROUPS):
        table_copy(g).start()

    def exchange_start(phase, tx, rx):
        n = tx.shape[0] // LON_DEV
        own = pl.ds(lon * n, n)
        peers(
            lambda peer: pltpu.make_async_remote_copy(
                tx.at[pl.ds(peer * n, n)],
                rx.at[own],
                send_sem.at[phase],
                recv_sem.at[phase],
                device_id={"lon": peer},
            ).start()
        )
        pltpu.make_async_copy(tx.at[own], rx.at[own], own_sem.at[phase]).start()

    def exchange_wait(phase, tx, rx):
        n = tx.shape[0] // LON_DEV
        own = pl.ds(lon * n, n)
        rest = pl.ds(0, (LON_DEV - 1) * n)
        pltpu.make_async_copy(tx.at[own], rx.at[own], own_sem.at[phase]).wait()
        pltpu.make_async_copy(rx.at[rest], rx.at[rest], recv_sem.at[phase]).wait()

    def exchange_sent(phase, tx):
        rest = pl.ds(0, (LON_DEV - 1) * (tx.shape[0] // LON_DEV))
        pltpu.make_async_copy(tx.at[rest], tx.at[rest], send_sem.at[phase]).wait()

    for copy in grid_copies:
        copy.wait()
    height, divergence, depth, tide, weight_row = grid
    weight = jnp.sum(
        jnp.where(
            iota((HALF, HALF), 0) == iota((HALF, HALF), 1),
            jnp.broadcast_to(weight_row[...], (HALF, HALF)),
            0.0,
        ),
        axis=1,
        keepdims=True,
    ) * (math.sqrt(NLON / NLAT) / MT / NLON)
    field_buf[...] = jnp.zeros_like(field_buf)
    fields = forcing_fields(height[...], divergence[...], depth[...], tide[...])
    for f in range(3):
        even, odd = fold(fields[f], weight)
        field_buf[0:HALF, 0:SPAN] = even
        field_buf[HALF:, 0:SPAN] = odd
        for h in range(2):
            tx1[pl.ds(2 * f + h, LON_DEV, stride=6), :] = field_buf[:, 128 * h : 128 * (h + 1)]

    pl.semaphore_wait(barrier, LON_DEV + 1)
    exchange_start(0, tx1, rx1)
    for copy in const_copies:
        copy.wait()
    spread, spread_t, twist, inner, back = (consts[n : n + 2] for n in (0, 2, 4, 6, 9))
    spread, spread_t = [r[...] for r in spread], [r[...] for r in spread_t]
    pick = consts[8]
    exchange_wait(0, tx1, rx1)

    for f in range(3):
        x = jnp.concatenate([rx1[pl.ds(2 * f + h, LON_DEV, stride=6), :] for h in range(2)], axis=1)
        tx2[pl.ds(f, LON_DEV, stride=3), :] = forward_row(x, spread, twist, inner, pick)
    exchange_start(1, tx2, rx2)
    exchange_wait(1, tx2, rx2)

    for f in range(3):
        wide = column_products(rx2[pl.ds(f, LON_DEV, stride=3), :], lon).astype(bf16)
        for g in range(GROUPS):
            for par in range(2):
                columns[g, 16 * (par * 3 + f) : 16 * (par * 3 + f + 1), :] = wide[
                    16 * g : 16 * (g + 1), 128 * par : 128 * (par + 1)
                ]

    def table_tail(g):
        last = table[pl.ds(GROUP * g, GROUP), :, SLOTS - 1 : SLOTS].reshape(128, 1).astype(f32)
        return jnp.where(iota((128, 128), 1) == 0, jnp.broadcast_to(last, (128, 128)), 0.0).astype(
            bf16
        )

    def table_tile(g, t):
        return table[pl.ds(GROUP * g, GROUP), :, TILE * t : TILE * (t + 1)].reshape(128, TILE)

    def tiles(g):
        for t in range(TILES):
            yield TILE * t, TILE, table_tile(g, t)
        yield TILE * TILES, 128, table_tail(g)

    def sibling_copy(g):
        return pltpu.make_async_remote_copy(
            sums.at[g, 1 - core],
            sibling_sums.at[g],
            lat_send.at[0, g],
            lat_recv.at[0, g],
            device_id=sibling,
        )

    def across_copy(g):
        return pltpu.make_async_remote_copy(
            chip_tx.at[g], chip_rx.at[g], lat_send.at[1, g], lat_recv.at[1, g], device_id=across
        )

    def share_copy(g):
        return pltpu.make_async_remote_copy(
            solved.at[g, core],
            solved.at[g, core],
            lat_send.at[2, g],
            lat_recv.at[2, g],
            device_id=sibling,
        )

    def forward_group(g):
        table_copy(g).wait()
        pair_first = lon * PAIRS + GROUP * g
        for first, width, rhs in tiles(g):
            both = partial_solve(dot(columns[g], rhs), pair_first, first)
            for field in range(2):
                sums[g, field, :, first : first + width] = both[field]
        sibling_copy(g).start()

    def sibling_sum(g):
        sibling_copy(g).wait_recv()
        total = sums[g, core] + sibling_sums[g]
        chip_tx[g] = total.astype(bf16)
        across_copy(g).start()
        sibling_sums[g] = total

    def across_sum(g):
        across_copy(g).wait_recv()
        total = sibling_sums[g] + chip_rx[g].astype(f32)
        solved[g, core] = total.astype(bf16)
        share_copy(g).start()

    def inverse_group(g):
        share_copy(g).wait_recv()
        pair_first = lon * PAIRS + GROUP * g
        total = None
        for first, width, rhs in tiles(g):
            both = [solved[g, field, :, first : first + width] for field in range(2)]
            term = dot_nt(rhs, inverse_rows(both, pair_first, first))
            total = term if total is None else total + term
        high, low = split(own_pair(total))
        order = lane_order(lon, g)
        message[...] += dot(high, order) + dot(low, order)

    def forward_step(t, _):
        forward_group(t)

        @pl.when(t > 0)
        def _():
            sibling_sum(t - 1)

        return 0

    lax.fori_loop(0, GROUPS, forward_step, 0)
    sibling_sum(GROUPS - 1)

    message[...] = jnp.zeros_like(message)
    across_sum(0)

    def inverse_step(t, _):
        @pl.when(t + 1 < GROUPS)
        def _():
            across_sum(t + 1)

        inverse_group(t)
        return 0

    lax.fori_loop(0, GROUPS, inverse_step, 0)

    for field in range(2):
        for side in range(2):
            tx4[pl.ds(2 * HALF * side + field, HALF, stride=2), :] = message[
                :, 128 * (2 * side + field) : 128 * (2 * side + field + 1)
            ]
    exchange_start(2, tx4, rx4)
    exchange_wait(2, tx4, rx4)

    for field in range(2):
        grid = inverse_row(rx4[pl.ds(field, LON_DEV, stride=2), :], spread_t, twist, back)
        for h in range(2):
            tx5[pl.ds(2 * field + h, LON_DEV, stride=4), :] = grid[:, 128 * h : 128 * (h + 1)]
    exchange_start(3, tx5, rx5)
    exchange_wait(3, tx5, rx5)
    for field, out in enumerate((out_height, out_divergence)):
        out[:, 0:128] = rx5[pl.ds(2 * field, LON_DEV, stride=4), :]
        out[:, 128:SPAN] = rx5[pl.ds(2 * field + 1, LON_DEV, stride=4), :][:, : SPAN - 128]

    for phase, tx in enumerate((tx1, tx2, tx4, tx5)):
        exchange_sent(phase, tx)
    for g in range(GROUPS):
        for copy in (sibling_copy, across_copy, share_copy):
            copy(g).wait_send()


def per_device(height, divergence, depth, tide, gauss_weight, legendre):
    consts = [jnp.asarray(t) for t in tables()]
    grid = (height, divergence, depth, tide, gauss_weight.reshape(1, HALF))
    vmem, hbm = pl.BlockSpec(memory_space=pltpu.VMEM), pl.BlockSpec(memory_space=pltpu.HBM)
    grid_shape = jax.ShapeDtypeStruct(height.shape, f32)

    def pair(rows):
        return [pltpu.VMEM((LON_DEV * rows, 128), f32)] * 2

    wide = 128 * pl.cdiv(SLOTS, 128)
    return pl.pallas_call(
        kernel,
        out_shape=(grid_shape, grid_shape),
        in_specs=[hbm] * (len(grid) + len(consts) + 1),
        out_specs=(vmem, vmem),
        scratch_shapes=[
            *[pltpu.VMEM(x.shape, x.dtype) for x in (*grid, *consts)],
            pltpu.VMEM((PAIRS, HALF, SLOTS), bf16),
            pltpu.VMEM((2 * HALF, 256), f32),
            *pair(6),
            *pair(3),
            *pair(2),
            *pair(4),
            pltpu.VMEM((GROUPS, 96, 128), bf16),
            pltpu.VMEM((GROUPS, 2, 8, wide), f32),
            pltpu.VMEM((GROUPS, 8, wide), f32),
            pltpu.VMEM((GROUPS, 8, wide), bf16),
            pltpu.VMEM((GROUPS, 8, wide), bf16),
            pltpu.VMEM((GROUPS, 2, 8, wide), bf16),
            pltpu.VMEM((HALF, 512), f32),
            pltpu.SemaphoreType.DMA((5 + CONSTS,)),
            pltpu.SemaphoreType.DMA((GROUPS,)),
            pltpu.SemaphoreType.DMA((4,)),
            pltpu.SemaphoreType.DMA((4,)),
            pltpu.SemaphoreType.DMA((4,)),
            pltpu.SemaphoreType.DMA((3, GROUPS)),
            pltpu.SemaphoreType.DMA((3, GROUPS)),
        ],
        compiler_params=pltpu.CompilerParams(
            collective_id=0, has_side_effects=True, vmem_limit_bytes=48 << 20
        ),
    )(*[pltpu.with_memory_space_constraint(x, pltpu.HBM) for x in (*grid, *consts, legendre)])


def solution(mesh):
    in_specs = (
        P("lat", "lon"),
        P("lat", "lon"),
        P("lat", "lon"),
        P("lat", "lon"),
        P("lat"),
        P("lon", "lat", None),
    )
    out_specs = (P("lat", "lon"), P("lat", "lon"))
    return jax.shard_map(
        per_device, mesh=mesh, in_specs=in_specs, out_specs=out_specs, check_vma=False
    )
```

```python
import math

import jax
import jax.numpy as jnp
import ml_dtypes
import numpy as np
from jax import lax
from jax.experimental import pallas as pl
from jax.experimental.pallas import tpu as pltpu
from jax.sharding import PartitionSpec as P

time_step = 0.5
drag_step = 0.1
coupling = 2.0
gravity_step = 4.0

f32, bf16 = jnp.float32, jnp.bfloat16

LON_DEV = 64
SPAN = 250
NLON = LON_DEV * SPAN
PAIRS = 28
MT = 2 * PAIRS * LON_DEV
SLOTS = MT + 1
HALF = 32
NLAT = 256
GROUP = 4
GROUPS = PAIRS // GROUP
TILE = 512
TILES = (SLOTS - 1) // TILE


def two_terms(table):
    high = table.astype(ml_dtypes.bfloat16)
    low = (table - high.astype(np.float64)).astype(ml_dtypes.bfloat16)
    return high, low


def tables():
    v, tau, s, j = np.arange(128), np.arange(16), np.arange(LON_DEV), np.arange(256)
    real = (j < SPAN).astype(np.float64)
    psi = 2 * np.pi * (np.outer(s, s) % LON_DEV) / LON_DEV
    spread = np.concatenate([np.cos(psi), -np.sin(psi)])
    first = np.stack([v, MT - v])
    theta = 2 * np.pi * ((first[:, :, None] * j) % NLON) / NLON
    twist_cos = (np.cos(theta) * real).reshape(256, 256).astype(np.float32)
    twist_sin = (np.sin(theta) * real).reshape(256, 256).astype(np.float32)

    def over_j(row, scale):
        phi = 2 * np.pi * ((128 * row[..., None] * j) % NLON) / NLON
        return scale * np.cos(phi) * real, scale * np.sin(phi) * real

    cos, sin = over_j(np.stack([tau, -tau]), 1)
    block = np.concatenate(
        [np.concatenate([cos, sin], axis=2), np.concatenate([-sin, cos], axis=2)], axis=1
    )
    inner = np.zeros((2, 512, 128))
    for member in range(2):
        inner[member, :, 32 * member : 32 * (member + 1)] = block[member].T
    inner = inner.reshape(1024, 128)
    row = np.stack([(PAIRS * s) // 128, (PAIRS * s + 1) // 128])
    row = np.concatenate([row, row + 1], axis=1)
    pick = (row[..., None] == tau).reshape(256, 16)
    cos, sin = over_j(row * np.array([[1], [-1]]), 2)
    back = np.concatenate(
        [np.concatenate([cos, sin], axis=2), np.concatenate([-sin, cos], axis=2)], axis=1
    ).reshape(512, 512)
    return (
        *two_terms(spread),
        *two_terms(np.ascontiguousarray(spread.T)),
        twist_cos,
        twist_sin,
        *two_terms(inner),
        pick.astype(ml_dtypes.bfloat16),
        *two_terms(back),
    )


def iota(shape, dim):
    return lax.broadcasted_iota(jnp.int32, shape, dim)


def dot(a, b):
    return lax.dot_general(a, b, (((1,), (0,)), ((), ())), preferred_element_type=f32)


def dot_nt(a, b):
    return lax.dot_general(a, b, (((1,), (1,)), ((), ())), preferred_element_type=f32)


def split(x):
    high = x.astype(bf16)
    return high, (x - high.astype(f32)).astype(bf16)


def three(product, a, b):
    return product(a[0], b[0]) + (product(a[0], b[1]) + product(a[1], b[0]))


def forcing_fields(height, divergence, depth, tide):
    return (
        height - time_step * (depth - 1.0) * divergence,
        divergence * (1.0 - drag_step / depth),
        tide,
    )


def fold(field, weight):
    north, south = field[:HALF], field[HALF:]
    return (north + south) * weight, (north - south) * weight


def lane_masks(member):
    lane = iota((LON_DEV, 128), 1)
    offset = (iota((LON_DEV, 128), 0) * PAIRS + member) & 127
    valid = ((lane - offset) & 127) < PAIRS
    return valid & (lane >= offset), valid & (lane < offset)


def twice(x):
    return jnp.concatenate([x, x], axis=0)


def forward_rows(x, spread, twist, inner, pick):
    y = dot(spread[0], x) + dot(spread[1], x)
    re, im = twice(y[:LON_DEV]), twice(y[LON_DEV:])
    waves = None
    for member in range(2):
        rows = slice(128 * member, 128 * (member + 1))
        cos, sin = (jnp.concatenate([t[rows]] * 3, axis=1) for t in twist)
        if member == 0:
            z = [re * cos + im * sin, im * cos - re * sin]
        else:
            z = [re * cos - im * sin, -(im * cos + re * sin)]
        z = [
            jnp.concatenate([part[:, 256 * f : 256 * (f + 1)] for f in range(3)], axis=0)
            for part in z
        ]
        cols = slice(512 * member, 512 * (member + 1))
        term = three(dot, split(jnp.concatenate(z, axis=1)), (inner[0][cols], inner[1][cols]))
        waves = term if waves is None else waves + term
    waves = [waves[128 * f : 128 * (f + 1)].T.astype(bf16) for f in range(3)]
    messages = [None] * 3
    for member in range(2):
        rows = slice(128 * member, 128 * (member + 1))
        first = 32 * member
        parts = [
            w[first + 16 * part : first + 16 * (part + 1)] for w in waves for part in range(2)
        ]
        values = dot(pick[rows], jnp.concatenate(parts, axis=1))
        straight, wrapped = lane_masks(member)
        for f in range(3):
            for part in range(2):
                slot = part * 2 + member
                cols = slice(128 * (2 * f + part), 128 * (2 * f + part + 1))
                own = jnp.where(
                    straight,
                    values[:LON_DEV, cols],
                    jnp.where(wrapped, values[LON_DEV:, cols], 0.0),
                )
                own = pltpu.roll(own, 32 * slot, 1) if slot else own
                messages[f] = own if messages[f] is None else messages[f] + own
    return messages


def pair_order(lon):
    r = iota((16 * GROUPS, 128), 0)
    member, part = (r >> 3) & 1, (r >> 2) & 1
    target = lon * PAIRS + 64 * part + 33 * member + 4 * (r >> 4) + (r & 3)
    return (((iota((16 * GROUPS, 128), 1) - target) & 127) == 0).astype(f32).astype(bf16)


def latitude_copies():
    source, lane = iota((64, 256), 0), iota((64, 256), 1)
    same = ((source >> 5) == (lane >> 7)) & ((source & 31) == (lane & 31))
    return same.astype(f32).astype(bf16)


def column_products(rows, order, copies):
    wide = dot(dot_nt(order, rows.astype(bf16)).astype(bf16), copies)
    own = ((iota(wide.shape, 1) >> 5) & 3) == (iota(wide.shape, 0) & 3)
    return jnp.where(own, wide, 0.0)


def slot_terms(shape, pair_first, slot_first):
    pair = pair_first + (iota(shape, 0) & 3)
    slot = slot_first + iota(shape, 1)
    upper = slot >= MT - pair
    odd = (jnp.where(upper, slot + pair, slot) & 1) == 1
    return pair, slot, upper, odd


def partial_solve(sums, pair_first, slot_first):
    shape = (8, sums.shape[1])
    pair, slot, upper, odd = slot_terms(shape, pair_first, slot_first)
    degree = jnp.where(upper, slot - 1, pair + slot)
    eigen = degree.astype(f32) * (degree + 1).astype(f32) / float(MT * MT)
    fields = []
    for field in range(3):
        block = [
            [sums[((par * 3 + field) * 2 + mem) * 8 :][:8] for mem in range(2)] for par in range(2)
        ]
        fields.append(
            jnp.where(
                upper,
                jnp.where(odd, block[1][1], block[0][1]),
                jnp.where(odd, block[1][0], block[0][0]),
            )
        )
    div_rhs = fields[1] - gravity_step * eigen * fields[2]
    height_spec = (fields[0] - time_step * div_rhs) / (1.0 + coupling * eigen)
    return height_spec, div_rhs + gravity_step * eigen * height_spec


def inverse_rows(solved, pair_first, slot_first):
    _, _, upper, odd = slot_terms(solved[0].shape, pair_first, slot_first)
    base = [x.astype(f32) for x in solved]
    rows = [jnp.where(upper, 0.0, x) for x in base] + [jnp.where(upper, x, 0.0) for x in base]
    rows += [jnp.where(odd, -x, x) for x in rows]
    return jnp.concatenate(rows, axis=0).astype(bf16)


def own_pair(products):
    lane = iota((HALF, 64), 1) & 3
    total = None
    for pair in range(GROUP):
        term = jnp.where(lane == pair, products[HALF * pair : HALF * (pair + 1)], 0.0)
        total = term if total is None else total + term
    return total


def lane_order(lon, group):
    r, c = iota((64, 512), 0), iota((64, 512), 1)
    member, part = (r >> 4) & 1, (r >> 2) & 1
    target = lon * PAIRS + 64 * part + 33 * member + 4 * group + (r & 3)
    same = ((r >> 5) == (c >> 8)) & (((r >> 3) & 1) == ((c >> 7) & 1))
    return (same & (((c - target) & 127) == 0)).astype(f32).astype(bf16)


def inverse_both(fields, spread_t, twist, back):
    mean = (iota((LON_DEV, 128), 0) == 0) & (iota((LON_DEV, 128), 1) == 0)
    total = None
    for member in range(2):
        straight, wrapped = lane_masks(member)
        turned = []
        for c in fields:
            stack = []
            for part in range(2):
                slot = part * 2 + member
                x = pltpu.roll(c, 128 - 32 * slot, 1) if slot else c
                if member == 0:
                    x = jnp.where(mean, 0.5 * x, x)
                stack += [jnp.where(straight, x, 0.0), jnp.where(wrapped, x, 0.0)]
            turned.append(jnp.concatenate(stack, axis=0).T)
        rows = slice(256 * member, 256 * (member + 1))
        b = three(dot, split(jnp.concatenate(turned, axis=0)), (back[0][rows], back[1][rows]))
        rows = slice(128 * member, 128 * (member + 1))
        cos, sin = twist[0][rows], twist[1][rows]
        z = [[], []]
        for f in range(2):
            re, im = b[128 * f : 128 * (f + 1), :256], b[128 * f : 128 * (f + 1), 256:]
            for part, x in enumerate((re * cos - im * sin, re * sin + im * cos)):
                z[part].append(x[:LON_DEV] + x[LON_DEV:])
        z = [jnp.concatenate(part, axis=1) for part in z]
        total = z if total is None else [total[0] + z[0], total[1] - z[1]]
    return three(dot, spread_t, split(jnp.concatenate(total, axis=0)))


CONSTS = 11
LAG = 2


def kernel(*refs):
    grid_in, refs = refs[:5], refs[5:]
    consts_in, refs = refs[:CONSTS], refs[CONSTS:]
    legendre, out_height, out_divergence, *refs = refs
    grid, refs = refs[:5], refs[5:]
    consts, refs = refs[:CONSTS], refs[CONSTS:]
    table, field_buf, row_buf, tx1, rx1, tx2, rx2, tx4, rx4, tx5, rx5, *refs = refs
    tails, order, copies, orders, columns, sums, sibling_sums, chip_tx, chip_rx, solved, message, *refs = refs
    in_sem, table_sem, send_sem, recv_sem, own_sem, lat_send, lat_recv = refs
    lon, lat = lax.axis_index("lon"), lax.axis_index("lat")
    core = lax.rem(lat, 2)
    sibling = {"lat": lat + 1 - 2 * core}
    across = {"lat": lax.rem(lat + 2, 4)}

    def peers(visit):
        x, z, y = lon >> 5, (lon >> 2) & 7, lon & 3
        for step in (4, 3, 5, 2, 6, 1, 7, 0):
            far = ((z + step) & 7) << 2

            def one(i, _):
                order = i >> 1
                turn = jnp.where(order == 0, 2, jnp.where(order == 1, 1, jnp.where(order == 2, 3, 0)))
                visit(((x ^ (1 - (i & 1))) << 5) | far | ((y + turn) & 3))
                return 0

            lax.fori_loop(0, 8 if step else 7, one, 0)

    def table_copy(g):
        rows = pl.ds(GROUP * g, GROUP)
        return pltpu.make_async_copy(legendre.at[rows], table.at[rows], table_sem.at[g])

    grid_copies = [
        pltpu.make_async_copy(a, b, in_sem.at[n]) for n, (a, b) in enumerate(zip(grid_in, grid))
    ]
    const_copies = [
        pltpu.make_async_copy(a, b, in_sem.at[5 + n])
        for n, (a, b) in enumerate(zip(consts_in, consts))
    ]
    for copy in grid_copies:
        copy.start()
    barrier = pltpu.get_barrier_semaphore()
    peers(lambda peer: pl.semaphore_signal(barrier, 1, device_id={"lon": peer}))
    pl.semaphore_signal(barrier, 1, device_id=sibling)
    pl.semaphore_signal(barrier, 1, device_id=across)
    for copy in const_copies:
        copy.start()
    for g in range(GROUPS):
        table_copy(g).start()

    def exchange_start(phase, tx, rx):
        n = tx.shape[0] // LON_DEV
        own = pl.ds(lon * n, n)
        peers(
            lambda peer: pltpu.make_async_remote_copy(
                tx.at[pl.ds(peer * n, n)],
                rx.at[own],
                send_sem.at[phase],
                recv_sem.at[phase],
                device_id={"lon": peer},
            ).start()
        )
        pltpu.make_async_copy(tx.at[own], rx.at[own], own_sem.at[phase]).start()

    def exchange_wait(phase, tx, rx):
        n = tx.shape[0] // LON_DEV
        own = pl.ds(lon * n, n)
        rest = pl.ds(0, (LON_DEV - 1) * n)
        pltpu.make_async_copy(tx.at[own], rx.at[own], own_sem.at[phase]).wait()
        pltpu.make_async_copy(rx.at[rest], rx.at[rest], recv_sem.at[phase]).wait()

    def exchange_sent(phase, tx):
        rest = pl.ds(0, (LON_DEV - 1) * (tx.shape[0] // LON_DEV))
        pltpu.make_async_copy(tx.at[rest], tx.at[rest], send_sem.at[phase]).wait()

    for copy in grid_copies:
        copy.wait()
    height, divergence, depth, tide, weight_row = grid
    weight = jnp.sum(
        jnp.where(
            iota((HALF, HALF), 0) == iota((HALF, HALF), 1),
            jnp.broadcast_to(weight_row[...], (HALF, HALF)),
            0.0,
        ),
        axis=1,
        keepdims=True,
    ) * (math.sqrt(NLON / NLAT) / MT / NLON)
    field_buf[...] = jnp.zeros_like(field_buf)
    fields = forcing_fields(height[...], divergence[...], depth[...], tide[...])
    for f in range(3):
        even, odd = fold(fields[f], weight)
        field_buf[0:HALF, 0:SPAN] = even
        field_buf[HALF:, 0:SPAN] = odd
        for h in range(2):
            row_buf[pl.ds(2 * f + h, LON_DEV, stride=6), :] = field_buf[:, 128 * h : 128 * (h + 1)]
    tx1[...] = row_buf[...].astype(bf16)

    pl.semaphore_wait(barrier, LON_DEV + 1)
    exchange_start(0, tx1, rx1)
    for copy in const_copies:
        copy.wait()
    spread, spread_t, twist, inner, back = (consts[n : n + 2] for n in (0, 2, 4, 6, 9))
    spread, spread_t = [r[...] for r in spread], [r[...] for r in spread_t]
    pick = consts[8]
    exchange_wait(0, tx1, rx1)

    row_buf[...] = rx1[...].astype(f32)
    x = jnp.concatenate([row_buf[pl.ds(c, LON_DEV, stride=6), :] for c in range(6)], axis=1)
    for f, rows in enumerate(forward_rows(x.astype(bf16), spread, twist, inner, pick)):
        tx2[pl.ds(f, LON_DEV, stride=3), :] = rows
    exchange_start(1, tx2, rx2)

    def prepare(g, _):
        table_copy(g).wait()
        last = table[pl.ds(GROUP * g, GROUP), :, SLOTS - 1 : SLOTS].reshape(128, 1).astype(f32)
        last = jnp.where(iota((128, 128), 1) == 0, jnp.broadcast_to(last, (128, 128)), 0.0)
        tails[g] = last.astype(bf16)
        orders[g] = lane_order(lon, g)
        return 0

    lax.fori_loop(0, GROUPS, prepare, 0)
    order[...] = pair_order(lon)
    copies[...] = latitude_copies()
    message[...] = jnp.zeros_like(message)
    exchange_wait(1, tx2, rx2)

    for f in range(3):
        rows = rx2[pl.ds(f, LON_DEV, stride=3), :]
        wide = column_products(rows, order[...], copies[...]).astype(bf16)
        for g in range(GROUPS):
            for par in range(2):
                columns[g, 16 * (par * 3 + f) : 16 * (par * 3 + f + 1), :] = wide[
                    16 * g : 16 * (g + 1), 128 * par : 128 * (par + 1)
                ]

    def table_tile(g, t):
        return table[pl.ds(GROUP * g, GROUP), :, TILE * t : TILE * (t + 1)].reshape(128, TILE)

    def tiles(g):
        for t in range(TILES):
            yield TILE * t, TILE, table_tile(g, t)
        yield TILE * TILES, 128, tails[g]

    def sibling_copy(g):
        return pltpu.make_async_remote_copy(
            sums.at[g, 1 - core],
            sibling_sums.at[g],
            lat_send.at[0, g],
            lat_recv.at[0, g],
            device_id=sibling,
        )

    def across_copy(g):
        return pltpu.make_async_remote_copy(
            chip_tx.at[g], chip_rx.at[g], lat_send.at[1, g], lat_recv.at[1, g], device_id=across
        )

    def share_copy(g):
        return pltpu.make_async_remote_copy(
            solved.at[g, core],
            solved.at[g, core],
            lat_send.at[2, g],
            lat_recv.at[2, g],
            device_id=sibling,
        )

    def forward_group(g):
        pair_first = lon * PAIRS + GROUP * g
        for first, width, rhs in tiles(g):
            both = partial_solve(dot(columns[g], rhs), pair_first, first)
            for field in range(2):
                sums[g, field, :, first : first + width] = both[field]
        sibling_copy(g).start()

    def sibling_sum(g):
        sibling_copy(g).wait_recv()
        total = sums[g, core] + sibling_sums[g]
        chip_tx[g] = total.astype(bf16)
        across_copy(g).start()
        sibling_sums[g] = total

    def across_sum(g):
        across_copy(g).wait_recv()
        total = sibling_sums[g] + chip_rx[g].astype(f32)
        solved[g, core] = total.astype(bf16)
        share_copy(g).start()

    def inverse_group(g):
        share_copy(g).wait_recv()
        pair_first = lon * PAIRS + GROUP * g
        total = None
        for first, width, rhs in tiles(g):
            both = [solved[g, field, :, first : first + width] for field in range(2)]
            term = dot_nt(rhs, inverse_rows(both, pair_first, first))
            total = term if total is None else total + term
        high, low = split(own_pair(total))
        message[...] += dot(high, orders[g]) + dot(low, orders[g])

    def forward_step(t, _):
        forward_group(t)

        @pl.when(t >= LAG)
        def _():
            sibling_sum(t - LAG)

        return 0

    lax.fori_loop(0, GROUPS, forward_step, 0)
    for g in range(GROUPS - LAG, GROUPS):
        sibling_sum(g)

    across_sum(0)

    def inverse_step(t, _):
        @pl.when(t + 1 < GROUPS)
        def _():
            across_sum(t + 1)

        inverse_group(t)
        return 0

    lax.fori_loop(0, GROUPS, inverse_step, 0)

    for field in range(2):
        for side in range(2):
            tx4[pl.ds(2 * HALF * side + field, HALF, stride=2), :] = message[
                :, 128 * (2 * side + field) : 128 * (2 * side + field + 1)
            ]
    exchange_start(2, tx4, rx4)
    exchange_wait(2, tx4, rx4)

    fields = [rx4[pl.ds(field, LON_DEV, stride=2), :] for field in range(2)]
    grid = inverse_both(fields, spread_t, twist, back)
    for c in range(4):
        tx5[pl.ds(c, LON_DEV, stride=4), :] = grid[:, 128 * c : 128 * (c + 1)]
    exchange_start(3, tx5, rx5)
    exchange_wait(3, tx5, rx5)
    for field, out in enumerate((out_height, out_divergence)):
        out[:, 0:128] = rx5[pl.ds(2 * field, LON_DEV, stride=4), :]
        out[:, 128:SPAN] = rx5[pl.ds(2 * field + 1, LON_DEV, stride=4), :][:, : SPAN - 128]

    for phase, tx in enumerate((tx1, tx2, tx4, tx5)):
        exchange_sent(phase, tx)
    for g in range(GROUPS):
        for copy in (sibling_copy, across_copy, share_copy):
            copy(g).wait_send()


def per_device(height, divergence, depth, tide, gauss_weight, legendre):
    consts = [jnp.asarray(t) for t in tables()]
    grid = (height, divergence, depth, tide, gauss_weight.reshape(1, HALF))
    vmem, hbm = pl.BlockSpec(memory_space=pltpu.VMEM), pl.BlockSpec(memory_space=pltpu.HBM)
    grid_shape = jax.ShapeDtypeStruct(height.shape, f32)

    def pair(rows, dtype=f32):
        return [pltpu.VMEM((LON_DEV * rows, 128), dtype)] * 2

    wide = 128 * pl.cdiv(SLOTS, 128)
    return pl.pallas_call(
        kernel,
        out_shape=(grid_shape, grid_shape),
        in_specs=[hbm] * (len(grid) + len(consts) + 1),
        out_specs=(vmem, vmem),
        scratch_shapes=[
            *[pltpu.VMEM(x.shape, x.dtype) for x in (*grid, *consts)],
            pltpu.VMEM((PAIRS, HALF, SLOTS), bf16),
            pltpu.VMEM((2 * HALF, 256), f32),
            pltpu.VMEM((LON_DEV * 6, 128), f32),
            *pair(6, bf16),
            *pair(3),
            *pair(2),
            *pair(4),
            pltpu.VMEM((GROUPS, 128, 128), bf16),
            pltpu.VMEM((16 * GROUPS, 128), bf16),
            pltpu.VMEM((2 * HALF, 256), bf16),
            pltpu.VMEM((GROUPS, 64, 512), bf16),
            pltpu.VMEM((GROUPS, 96, 128), bf16),
            pltpu.VMEM((GROUPS, 2, 8, wide), f32),
            pltpu.VMEM((GROUPS, 8, wide), f32),
            pltpu.VMEM((GROUPS, 8, wide), bf16),
            pltpu.VMEM((GROUPS, 8, wide), bf16),
            pltpu.VMEM((GROUPS, 2, 8, wide), bf16),
            pltpu.VMEM((HALF, 512), f32),
            pltpu.SemaphoreType.DMA((5 + CONSTS,)),
            pltpu.SemaphoreType.DMA((GROUPS,)),
            pltpu.SemaphoreType.DMA((4,)),
            pltpu.SemaphoreType.DMA((4,)),
            pltpu.SemaphoreType.DMA((4,)),
            pltpu.SemaphoreType.DMA((3, GROUPS)),
            pltpu.SemaphoreType.DMA((3, GROUPS)),
        ],
        compiler_params=pltpu.CompilerParams(
            collective_id=0, has_side_effects=True, vmem_limit_bytes=48 << 20
        ),
    )(*[pltpu.with_memory_space_constraint(x, pltpu.HBM) for x in (*grid, *consts, legendre)])


def solution(mesh):
    in_specs = (
        P("lat", "lon"),
        P("lat", "lon"),
        P("lat", "lon"),
        P("lat", "lon"),
        P("lat"),
        P("lon", "lat", None),
    )
    out_specs = (P("lat", "lon"), P("lat", "lon"))
    return jax.shard_map(
        per_device, mesh=mesh, in_specs=in_specs, out_specs=out_specs, check_vma=False
    )
```

```python
import math

import jax
import jax.numpy as jnp
import ml_dtypes
import numpy as np
from jax import lax
from jax.experimental import pallas as pl
from jax.experimental.pallas import tpu as pltpu
from jax.sharding import PartitionSpec as P

time_step = 0.5
drag_step = 0.1
coupling = 2.0
gravity_step = 4.0

f32, bf16 = jnp.float32, jnp.bfloat16

LON_DEV = 64
SPAN = 250
NLON = LON_DEV * SPAN
PAIRS = 28
MT = 2 * PAIRS * LON_DEV
SLOTS = MT + 1
HALF = 32
NLAT = 256
GROUP = 4
GROUPS = PAIRS // GROUP
TILE = 512
TILES = (SLOTS - 1) // TILE


def two_terms(table):
    high = table.astype(ml_dtypes.bfloat16)
    low = (table - high.astype(np.float64)).astype(ml_dtypes.bfloat16)
    return high, low


def tables():
    v, tau, s, j = np.arange(128), np.arange(16), np.arange(LON_DEV), np.arange(256)
    real = (j < SPAN).astype(np.float64)
    psi = 2 * np.pi * (np.outer(s, s) % LON_DEV) / LON_DEV
    spread = np.concatenate([np.cos(psi), -np.sin(psi)])
    first = np.stack([v, MT - v])
    theta = 2 * np.pi * ((first[:, :, None] * j) % NLON) / NLON
    twist_cos = (np.cos(theta) * real).reshape(256, 256).astype(np.float32)
    twist_sin = (np.sin(theta) * real).reshape(256, 256).astype(np.float32)

    def over_j(row, scale):
        phi = 2 * np.pi * ((128 * row[..., None] * j) % NLON) / NLON
        return scale * np.cos(phi) * real, scale * np.sin(phi) * real

    cos, sin = over_j(np.stack([tau, -tau]), 1)
    block = np.concatenate(
        [np.concatenate([cos, sin], axis=2), np.concatenate([-sin, cos], axis=2)], axis=1
    )
    inner = np.zeros((2, 512, 128))
    for member in range(2):
        inner[member, :, 32 * member : 32 * (member + 1)] = block[member].T
    inner = inner.reshape(1024, 128)
    row = np.stack([(PAIRS * s) // 128, (PAIRS * s + 1) // 128])
    row = np.concatenate([row, row + 1], axis=1)
    pick = (row[..., None] == tau).reshape(256, 16)
    cos, sin = over_j(row * np.array([[1], [-1]]), 2)
    back = np.concatenate(
        [np.concatenate([cos, sin], axis=2), np.concatenate([-sin, cos], axis=2)], axis=1
    ).reshape(512, 512)
    return (
        *two_terms(spread),
        *two_terms(np.ascontiguousarray(spread.T)),
        twist_cos,
        twist_sin,
        *two_terms(inner),
        pick.astype(ml_dtypes.bfloat16),
        *two_terms(back),
    )


def iota(shape, dim):
    return lax.broadcasted_iota(jnp.int32, shape, dim)


def dot(a, b):
    return lax.dot_general(a, b, (((1,), (0,)), ((), ())), preferred_element_type=f32)


def dot_nt(a, b):
    return lax.dot_general(a, b, (((1,), (1,)), ((), ())), preferred_element_type=f32)


def split(x):
    high = x.astype(bf16)
    return high, (x - high.astype(f32)).astype(bf16)


def three(product, a, b):
    return product(a[0], b[0]) + (product(a[0], b[1]) + product(a[1], b[0]))


def forcing_fields(height, divergence, depth, tide):
    return (
        height - time_step * (depth - 1.0) * divergence,
        divergence * (1.0 - drag_step / depth),
        tide,
    )


def fold(field, weight):
    north, south = field[:HALF], field[HALF:]
    return (north + south) * weight, (north - south) * weight


def lane_masks(member):
    lane = iota((LON_DEV, 128), 1)
    offset = (iota((LON_DEV, 128), 0) * PAIRS + member) & 127
    valid = ((lane - offset) & 127) < PAIRS
    return valid & (lane >= offset), valid & (lane < offset)


def twice(x):
    return jnp.concatenate([x, x], axis=0)


def forward_rows(x, spread, twist, inner, pick):
    y = dot(spread[0], x) + dot(spread[1], x)
    re, im = twice(y[:LON_DEV]), twice(y[LON_DEV:])
    waves = None
    for member in range(2):
        rows = slice(128 * member, 128 * (member + 1))
        cos, sin = (jnp.concatenate([t[rows]] * 3, axis=1) for t in twist)
        if member == 0:
            z = [re * cos + im * sin, im * cos - re * sin]
        else:
            z = [re * cos - im * sin, -(im * cos + re * sin)]
        z = [
            jnp.concatenate([part[:, 256 * f : 256 * (f + 1)] for f in range(3)], axis=0)
            for part in z
        ]
        cols = slice(512 * member, 512 * (member + 1))
        term = three(dot, split(jnp.concatenate(z, axis=1)), (inner[0][cols], inner[1][cols]))
        waves = term if waves is None else waves + term
    waves = [waves[128 * f : 128 * (f + 1)].T.astype(bf16) for f in range(3)]
    messages = [None] * 3
    for member in range(2):
        rows = slice(128 * member, 128 * (member + 1))
        first = 32 * member
        parts = [
            w[first + 16 * part : first + 16 * (part + 1)] for w in waves for part in range(2)
        ]
        values = dot(pick[rows], jnp.concatenate(parts, axis=1))
        straight, wrapped = lane_masks(member)
        for f in range(3):
            for part in range(2):
                slot = part * 2 + member
                cols = slice(128 * (2 * f + part), 128 * (2 * f + part + 1))
                own = jnp.where(
                    straight,
                    values[:LON_DEV, cols],
                    jnp.where(wrapped, values[LON_DEV:, cols], 0.0),
                )
                own = pltpu.roll(own, 32 * slot, 1) if slot else own
                messages[f] = own if messages[f] is None else messages[f] + own
    return messages


def pair_order(lon):
    r = iota((16 * GROUPS, 128), 0)
    member, part = (r >> 3) & 1, (r >> 2) & 1
    target = lon * PAIRS + 64 * part + 33 * member + 4 * (r >> 4) + (r & 3)
    return (((iota((16 * GROUPS, 128), 1) - target) & 127) == 0).astype(f32).astype(bf16)


def latitude_copies():
    source, lane = iota((64, 256), 0), iota((64, 256), 1)
    same = ((source >> 5) == (lane >> 7)) & ((source & 31) == (lane & 31))
    return same.astype(f32).astype(bf16)


def column_products(rows, order, copies):
    wide = dot(dot_nt(order, rows.astype(bf16)).astype(bf16), copies)
    own = ((iota(wide.shape, 1) >> 5) & 3) == (iota(wide.shape, 0) & 3)
    return jnp.where(own, wide, 0.0)


def slot_terms(shape, pair_first, slot_first):
    pair = pair_first + (iota(shape, 0) & 3)
    slot = slot_first + iota(shape, 1)
    upper = slot >= MT - pair
    odd = (jnp.where(upper, slot + pair, slot) & 1) == 1
    return pair, slot, upper, odd


def partial_solve(sums, pair_first, slot_first):
    shape = (8, sums.shape[1])
    pair, slot, upper, odd = slot_terms(shape, pair_first, slot_first)
    degree = jnp.where(upper, slot - 1, pair + slot)
    eigen = degree.astype(f32) * (degree + 1).astype(f32) / float(MT * MT)
    fields = []
    for field in range(3):
        block = [
            [sums[((par * 3 + field) * 2 + mem) * 8 :][:8] for mem in range(2)] for par in range(2)
        ]
        fields.append(
            jnp.where(
                upper,
                jnp.where(odd, block[1][1], block[0][1]),
                jnp.where(odd, block[1][0], block[0][0]),
            )
        )
    div_rhs = fields[1] - gravity_step * eigen * fields[2]
    height_spec = (fields[0] - time_step * div_rhs) / (1.0 + coupling * eigen)
    return height_spec, div_rhs + gravity_step * eigen * height_spec


def inverse_rows(solved, pair_first, slot_first):
    _, _, upper, odd = slot_terms(solved[0].shape, pair_first, slot_first)
    base = [x.astype(f32) for x in solved]
    rows = [jnp.where(upper, 0.0, x) for x in base] + [jnp.where(upper, x, 0.0) for x in base]
    rows += [jnp.where(odd, -x, x) for x in rows]
    return jnp.concatenate(rows, axis=0).astype(bf16)


def own_pair(products):
    lane = iota((HALF, 64), 1) & 3
    total = None
    for pair in range(GROUP):
        term = jnp.where(lane == pair, products[HALF * pair : HALF * (pair + 1)], 0.0)
        total = term if total is None else total + term
    return total


def lane_order(lon, group):
    r, c = iota((64, 512), 0), iota((64, 512), 1)
    member, part = (r >> 4) & 1, (r >> 2) & 1
    target = lon * PAIRS + 64 * part + 33 * member + 4 * group + (r & 3)
    same = ((r >> 5) == (c >> 8)) & (((r >> 3) & 1) == ((c >> 7) & 1))
    return (same & (((c - target) & 127) == 0)).astype(f32).astype(bf16)


def inverse_both(fields, spread_t, twist, back):
    mean = (iota((LON_DEV, 128), 0) == 0) & (iota((LON_DEV, 128), 1) == 0)
    total = None
    for member in range(2):
        straight, wrapped = lane_masks(member)
        turned = []
        for c in fields:
            stack = []
            for part in range(2):
                slot = part * 2 + member
                x = pltpu.roll(c, 128 - 32 * slot, 1) if slot else c
                if member == 0:
                    x = jnp.where(mean, 0.5 * x, x)
                stack += [jnp.where(straight, x, 0.0), jnp.where(wrapped, x, 0.0)]
            turned.append(jnp.concatenate(stack, axis=0).T)
        rows = slice(256 * member, 256 * (member + 1))
        b = three(dot, split(jnp.concatenate(turned, axis=0)), (back[0][rows], back[1][rows]))
        rows = slice(128 * member, 128 * (member + 1))
        cos, sin = twist[0][rows], twist[1][rows]
        z = [[], []]
        for f in range(2):
            re, im = b[128 * f : 128 * (f + 1), :256], b[128 * f : 128 * (f + 1), 256:]
            for part, x in enumerate((re * cos - im * sin, re * sin + im * cos)):
                z[part].append(x[:LON_DEV] + x[LON_DEV:])
        z = [jnp.concatenate(part, axis=1) for part in z]
        total = z if total is None else [total[0] + z[0], total[1] - z[1]]
    return three(dot, spread_t, split(jnp.concatenate(total, axis=0)))


CONSTS = 11
LAG = 2


def kernel(*refs):
    grid_in, refs = refs[:5], refs[5:]
    consts_in, refs = refs[:CONSTS], refs[CONSTS:]
    legendre, out, *refs = refs
    grid, refs = refs[:5], refs[5:]
    consts, refs = refs[:CONSTS], refs[CONSTS:]
    table, field_buf, row_buf, tx1, rx1, tx2, rx2, tx4, rx4, tx5, rx5, *refs = refs
    tails, order, copies, orders, columns, sums, sibling_sums, chip_tx, chip_rx, solved, message, *refs = refs
    in_sem, table_sem, send_sem, recv_sem, own_sem, lat_send, lat_recv = refs
    lon, lat = lax.axis_index("lon"), lax.axis_index("lat")
    core = lax.rem(lat, 2)
    sibling = {"lat": lat + 1 - 2 * core}
    across = {"lat": lax.rem(lat + 2, 4)}

    def peers(visit):
        x, z, y = lon >> 5, (lon >> 2) & 7, lon & 3
        for step in (4, 3, 5, 2, 6, 1, 7, 0):
            far = ((z + step) & 7) << 2

            def one(i, _):
                order = i >> 1
                turn = jnp.where(order == 0, 2, jnp.where(order == 1, 1, jnp.where(order == 2, 3, 0)))
                visit(((x ^ (1 - (i & 1))) << 5) | far | ((y + turn) & 3))
                return 0

            lax.fori_loop(0, 8 if step else 7, one, 0)

    def table_copy(g):
        rows = pl.ds(GROUP * g, GROUP)
        return pltpu.make_async_copy(legendre.at[rows], table.at[rows], table_sem.at[g])

    grid_copies = [
        pltpu.make_async_copy(a, b, in_sem.at[n]) for n, (a, b) in enumerate(zip(grid_in, grid))
    ]
    const_copies = [
        pltpu.make_async_copy(a, b, in_sem.at[5 + n])
        for n, (a, b) in enumerate(zip(consts_in, consts))
    ]
    for copy in grid_copies:
        copy.start()
    barrier = pltpu.get_barrier_semaphore()
    peers(lambda peer: pl.semaphore_signal(barrier, 1, device_id={"lon": peer}))
    pl.semaphore_signal(barrier, 1, device_id=sibling)
    pl.semaphore_signal(barrier, 1, device_id=across)
    for copy in const_copies:
        copy.start()
    for g in range(GROUPS):
        table_copy(g).start()

    def exchange_start(phase, tx, rx):
        n = tx.shape[0] // LON_DEV
        own = pl.ds(lon * n, n)
        peers(
            lambda peer: pltpu.make_async_remote_copy(
                tx.at[pl.ds(peer * n, n)],
                rx.at[own],
                send_sem.at[phase],
                recv_sem.at[phase],
                device_id={"lon": peer},
            ).start()
        )
        pltpu.make_async_copy(tx.at[own], rx.at[own], own_sem.at[phase]).start()

    def exchange_wait(phase, tx, rx):
        n = tx.shape[0] // LON_DEV
        own = pl.ds(lon * n, n)
        rest = pl.ds(0, (LON_DEV - 1) * n)
        pltpu.make_async_copy(tx.at[own], rx.at[own], own_sem.at[phase]).wait()
        pltpu.make_async_copy(rx.at[rest], rx.at[rest], recv_sem.at[phase]).wait()

    def exchange_sent(phase, tx):
        rest = pl.ds(0, (LON_DEV - 1) * (tx.shape[0] // LON_DEV))
        pltpu.make_async_copy(tx.at[rest], tx.at[rest], send_sem.at[phase]).wait()

    for copy in grid_copies:
        copy.wait()
    height, divergence, depth, tide, weight_row = grid
    weight = jnp.sum(
        jnp.where(
            iota((HALF, HALF), 0) == iota((HALF, HALF), 1),
            jnp.broadcast_to(weight_row[...], (HALF, HALF)),
            0.0,
        ),
        axis=1,
        keepdims=True,
    ) * (math.sqrt(NLON / NLAT) / MT / NLON)
    field_buf[...] = jnp.zeros_like(field_buf)
    fields = forcing_fields(height[...], divergence[...], depth[...], tide[...])
    for f in range(3):
        even, odd = fold(fields[f], weight)
        field_buf[0:HALF, 0:SPAN] = even
        field_buf[HALF:, 0:SPAN] = odd
        for h in range(2):
            row_buf[pl.ds(2 * f + h, LON_DEV, stride=6), :] = field_buf[:, 128 * h : 128 * (h + 1)]
    tx1[...] = row_buf[...].astype(bf16)

    pl.semaphore_wait(barrier, LON_DEV + 1)
    exchange_start(0, tx1, rx1)
    for copy in const_copies:
        copy.wait()
    spread, spread_t, twist, inner, back = (consts[n : n + 2] for n in (0, 2, 4, 6, 9))
    spread, spread_t = [r[...] for r in spread], [r[...] for r in spread_t]
    pick = consts[8]
    exchange_wait(0, tx1, rx1)

    row_buf[...] = rx1[...].astype(f32)
    x = jnp.concatenate([row_buf[pl.ds(c, LON_DEV, stride=6), :] for c in range(6)], axis=1)
    for f, rows in enumerate(forward_rows(x.astype(bf16), spread, twist, inner, pick)):
        tx2[pl.ds(f, LON_DEV, stride=3), :] = rows
    exchange_start(1, tx2, rx2)

    def prepare(g, _):
        table_copy(g).wait()
        last = table[pl.ds(GROUP * g, GROUP), :, SLOTS - 1 : SLOTS].reshape(128, 1).astype(f32)
        last = jnp.where(iota((128, 128), 1) == 0, jnp.broadcast_to(last, (128, 128)), 0.0)
        tails[g] = last.astype(bf16)
        orders[g] = lane_order(lon, g)
        return 0

    lax.fori_loop(0, GROUPS, prepare, 0)
    order[...] = pair_order(lon)
    copies[...] = latitude_copies()
    message[...] = jnp.zeros_like(message)
    exchange_wait(1, tx2, rx2)

    for f in range(3):
        rows = rx2[pl.ds(f, LON_DEV, stride=3), :]
        wide = column_products(rows, order[...], copies[...]).astype(bf16)
        for g in range(GROUPS):
            for par in range(2):
                columns[g, 16 * (par * 3 + f) : 16 * (par * 3 + f + 1), :] = wide[
                    16 * g : 16 * (g + 1), 128 * par : 128 * (par + 1)
                ]

    def table_tile(g, t):
        return table[pl.ds(GROUP * g, GROUP), :, TILE * t : TILE * (t + 1)].reshape(128, TILE)

    def tiles(g):
        for t in range(TILES):
            yield TILE * t, TILE, table_tile(g, t)
        yield TILE * TILES, 128, tails[g]

    def sibling_copy(g):
        return pltpu.make_async_remote_copy(
            sums.at[g, 1 - core],
            sibling_sums.at[g],
            lat_send.at[0, g],
            lat_recv.at[0, g],
            device_id=sibling,
        )

    def across_copy(g):
        return pltpu.make_async_remote_copy(
            chip_tx.at[g], chip_rx.at[g], lat_send.at[1, g], lat_recv.at[1, g], device_id=across
        )

    def share_copy(g):
        return pltpu.make_async_remote_copy(
            solved.at[g, core],
            solved.at[g, core],
            lat_send.at[2, g],
            lat_recv.at[2, g],
            device_id=sibling,
        )

    def forward_group(g):
        pair_first = lon * PAIRS + GROUP * g
        for first, width, rhs in tiles(g):
            both = partial_solve(dot(columns[g], rhs), pair_first, first)
            for field in range(2):
                sums[g, field, :, first : first + width] = both[field]
        sibling_copy(g).start()

    def sibling_sum(g):
        sibling_copy(g).wait_recv()
        total = sums[g, core] + sibling_sums[g]
        chip_tx[g] = total.astype(bf16)
        across_copy(g).start()
        sibling_sums[g] = total

    def across_sum(g):
        across_copy(g).wait_recv()
        total = sibling_sums[g] + chip_rx[g].astype(f32)
        solved[g, core] = total.astype(bf16)
        share_copy(g).start()

    def inverse_group(g):
        share_copy(g).wait_recv()
        pair_first = lon * PAIRS + GROUP * g
        total = None
        for first, width, rhs in tiles(g):
            both = [solved[g, field, :, first : first + width] for field in range(2)]
            term = dot_nt(rhs, inverse_rows(both, pair_first, first))
            total = term if total is None else total + term
        high, low = split(own_pair(total))
        message[...] += dot(high, orders[g]) + dot(low, orders[g])

    def forward_step(t, _):
        forward_group(t)

        @pl.when(t >= LAG)
        def _():
            sibling_sum(t - LAG)

        return 0

    lax.fori_loop(0, GROUPS, forward_step, 0)
    for g in range(GROUPS - LAG, GROUPS):
        sibling_sum(g)

    across_sum(0)

    def inverse_step(t, _):
        @pl.when(t + 1 < GROUPS)
        def _():
            across_sum(t + 1)

        inverse_group(t)
        return 0

    lax.fori_loop(0, GROUPS, inverse_step, 0)

    for field in range(2):
        for side in range(2):
            tx4[pl.ds(2 * HALF * side + field, HALF, stride=2), :] = message[
                :, 128 * (2 * side + field) : 128 * (2 * side + field + 1)
            ]
    exchange_start(2, tx4, rx4)
    exchange_wait(2, tx4, rx4)

    fields = [rx4[pl.ds(field, LON_DEV, stride=2), :] for field in range(2)]
    grid = inverse_both(fields, spread_t, twist, back)
    for c in range(4):
        tx5[pl.ds(c, LON_DEV, stride=4), :] = grid[:, 128 * c : 128 * (c + 1)]
    exchange_start(3, tx5, rx5)
    exchange_wait(3, tx5, rx5)
    for field in range(2):
        for h in range(2):
            out[field, :, 128 * h : 128 * (h + 1)] = rx5[pl.ds(2 * field + h, LON_DEV, stride=4), :]

    for phase, tx in enumerate((tx1, tx2, tx4, tx5)):
        exchange_sent(phase, tx)
    for g in range(GROUPS):
        for copy in (sibling_copy, across_copy, share_copy):
            copy(g).wait_send()


def per_device(height, divergence, depth, tide, gauss_weight, legendre):
    consts = [jnp.asarray(t) for t in tables()]
    grid = (height, divergence, depth, tide, gauss_weight.reshape(1, HALF))
    vmem, hbm = pl.BlockSpec(memory_space=pltpu.VMEM), pl.BlockSpec(memory_space=pltpu.HBM)
    grid_shape = jax.ShapeDtypeStruct(height.shape, f32)

    def pair(rows, dtype=f32):
        return [pltpu.VMEM((LON_DEV * rows, 128), dtype)] * 2

    wide = 128 * pl.cdiv(SLOTS, 128)
    raw = pl.pallas_call(
        kernel,
        out_shape=jax.ShapeDtypeStruct((2, LON_DEV, 256), f32),
        in_specs=[hbm] * (len(grid) + len(consts) + 1),
        out_specs=vmem,
        scratch_shapes=[
            *[pltpu.VMEM(x.shape, x.dtype) for x in (*grid, *consts)],
            pltpu.VMEM((PAIRS, HALF, SLOTS), bf16),
            pltpu.VMEM((2 * HALF, 256), f32),
            pltpu.VMEM((LON_DEV * 6, 128), f32),
            *pair(6, bf16),
            *pair(3),
            *pair(2),
            *pair(4),
            pltpu.VMEM((GROUPS, 128, 128), bf16),
            pltpu.VMEM((16 * GROUPS, 128), bf16),
            pltpu.VMEM((2 * HALF, 256), bf16),
            pltpu.VMEM((GROUPS, 64, 512), bf16),
            pltpu.VMEM((GROUPS, 96, 128), bf16),
            pltpu.VMEM((GROUPS, 2, 8, wide), f32),
            pltpu.VMEM((GROUPS, 8, wide), f32),
            pltpu.VMEM((GROUPS, 8, wide), bf16),
            pltpu.VMEM((GROUPS, 8, wide), bf16),
            pltpu.VMEM((GROUPS, 2, 8, wide), bf16),
            pltpu.VMEM((HALF, 512), f32),
            pltpu.SemaphoreType.DMA((5 + CONSTS,)),
            pltpu.SemaphoreType.DMA((GROUPS,)),
            pltpu.SemaphoreType.DMA((4,)),
            pltpu.SemaphoreType.DMA((4,)),
            pltpu.SemaphoreType.DMA((4,)),
            pltpu.SemaphoreType.DMA((3, GROUPS)),
            pltpu.SemaphoreType.DMA((3, GROUPS)),
        ],
        compiler_params=pltpu.CompilerParams(
            collective_id=0, has_side_effects=True, vmem_limit_bytes=48 << 20
        ),
    )(*[pltpu.with_memory_space_constraint(x, pltpu.HBM) for x in (*grid, *consts, legendre)])
    return raw[0, :, :SPAN], raw[1, :, :SPAN]


def solution(mesh):
    in_specs = (
        P("lat", "lon"),
        P("lat", "lon"),
        P("lat", "lon"),
        P("lat", "lon"),
        P("lat"),
        P("lon", "lat", None),
    )
    out_specs = (P("lat", "lon"), P("lat", "lon"))
    return jax.shard_map(
        per_device, mesh=mesh, in_specs=in_specs, out_specs=out_specs, check_vma=False
    )
```

```python
import math

import jax
import jax.numpy as jnp
import ml_dtypes
import numpy as np
from jax import lax
from jax.experimental import pallas as pl
from jax.experimental.pallas import tpu as pltpu
from jax.sharding import PartitionSpec as P

time_step = 0.5
drag_step = 0.1
coupling = 2.0
gravity_step = 4.0

f32, bf16 = jnp.float32, jnp.bfloat16

LON_DEV = 64
SPAN = 250
NLON = LON_DEV * SPAN
PAIRS = 28
MT = 2 * PAIRS * LON_DEV
SLOTS = MT + 1
HALF = 32
NLAT = 256
GROUP = 4
GROUPS = PAIRS // GROUP
TILE = 512
TILES = (SLOTS - 1) // TILE


def two_terms(table):
    high = table.astype(ml_dtypes.bfloat16)
    low = (table - high.astype(np.float64)).astype(ml_dtypes.bfloat16)
    return high, low


def tables():
    v, tau, s, j = np.arange(128), np.arange(16), np.arange(LON_DEV), np.arange(256)
    real = (j < SPAN).astype(np.float64)
    psi = 2 * np.pi * (np.outer(s, s) % LON_DEV) / LON_DEV
    spread = np.concatenate([np.cos(psi), -np.sin(psi)])
    first = np.stack([v, MT - v])
    theta = 2 * np.pi * ((first[:, :, None] * j) % NLON) / NLON
    twist_cos = (np.cos(theta) * real).reshape(256, 256).astype(np.float32)
    twist_sin = (np.sin(theta) * real).reshape(256, 256).astype(np.float32)

    def over_j(row, scale):
        phi = 2 * np.pi * ((128 * row[..., None] * j) % NLON) / NLON
        return scale * np.cos(phi) * real, scale * np.sin(phi) * real

    cos, sin = over_j(np.stack([tau, -tau]), 1)
    block = np.concatenate(
        [np.concatenate([cos, sin], axis=2), np.concatenate([-sin, cos], axis=2)], axis=1
    )
    inner = np.zeros((2, 512, 128))
    for member in range(2):
        inner[member, :, 32 * member : 32 * (member + 1)] = block[member].T
    inner = inner.reshape(1024, 128)
    row = np.stack([(PAIRS * s) // 128, (PAIRS * s + 1) // 128])
    row = np.concatenate([row, row + 1], axis=1)
    pick = (row[..., None] == tau).reshape(256, 16)
    cos, sin = over_j(row * np.array([[1], [-1]]), 2)
    back = np.concatenate(
        [np.concatenate([cos, sin], axis=2), np.concatenate([-sin, cos], axis=2)], axis=1
    ).reshape(512, 512)
    return (
        *two_terms(spread),
        *two_terms(np.ascontiguousarray(spread.T)),
        twist_cos,
        twist_sin,
        *two_terms(inner),
        pick.astype(ml_dtypes.bfloat16),
        *two_terms(back),
    )


def iota(shape, dim):
    return lax.broadcasted_iota(jnp.int32, shape, dim)


def dot(a, b):
    return lax.dot_general(a, b, (((1,), (0,)), ((), ())), preferred_element_type=f32)


def dot_nt(a, b):
    return lax.dot_general(a, b, (((1,), (1,)), ((), ())), preferred_element_type=f32)


def split(x):
    high = x.astype(bf16)
    return high, (x - high.astype(f32)).astype(bf16)


def three(product, a, b):
    return product(a[0], b[0]) + (product(a[0], b[1]) + product(a[1], b[0]))


def forcing_fields(height, divergence, depth, tide):
    return (
        height - time_step * (depth - 1.0) * divergence,
        divergence * (1.0 - drag_step / depth),
        tide,
    )


def fold(field, weight):
    north, south = field[:HALF], field[HALF:]
    return (north + south) * weight, (north - south) * weight


def lane_masks(member):
    lane = iota((LON_DEV, 128), 1)
    offset = (iota((LON_DEV, 128), 0) * PAIRS + member) & 127
    valid = ((lane - offset) & 127) < PAIRS
    return valid & (lane >= offset), valid & (lane < offset)


def twice(x):
    return jnp.concatenate([x, x], axis=0)


def forward_rows(x, spread, twist, inner, pick):
    y = dot(spread[0], x) + dot(spread[1], x)
    re, im = twice(y[:LON_DEV]), twice(y[LON_DEV:])
    waves = None
    for member in range(2):
        rows = slice(128 * member, 128 * (member + 1))
        cos, sin = (jnp.concatenate([t[rows]] * 3, axis=1) for t in twist)
        if member == 0:
            z = [re * cos + im * sin, im * cos - re * sin]
        else:
            z = [re * cos - im * sin, -(im * cos + re * sin)]
        z = [
            jnp.concatenate([part[:, 256 * f : 256 * (f + 1)] for f in range(3)], axis=0)
            for part in z
        ]
        cols = slice(512 * member, 512 * (member + 1))
        term = three(dot, split(jnp.concatenate(z, axis=1)), (inner[0][cols], inner[1][cols]))
        waves = term if waves is None else waves + term
    waves = [waves[128 * f : 128 * (f + 1)].T.astype(bf16) for f in range(3)]
    messages = [None] * 3
    for member in range(2):
        rows = slice(128 * member, 128 * (member + 1))
        first = 32 * member
        parts = [
            w[first + 16 * part : first + 16 * (part + 1)] for w in waves for part in range(2)
        ]
        values = dot(pick[rows], jnp.concatenate(parts, axis=1))
        straight, wrapped = lane_masks(member)
        for f in range(3):
            for part in range(2):
                slot = part * 2 + member
                cols = slice(128 * (2 * f + part), 128 * (2 * f + part + 1))
                own = jnp.where(
                    straight,
                    values[:LON_DEV, cols],
                    jnp.where(wrapped, values[LON_DEV:, cols], 0.0),
                )
                own = pltpu.roll(own, 32 * slot, 1) if slot else own
                messages[f] = own if messages[f] is None else messages[f] + own
    return messages


def pair_order(lon):
    r = iota((16 * GROUPS, 128), 0)
    member, part = (r >> 3) & 1, (r >> 2) & 1
    target = lon * PAIRS + 64 * part + 33 * member + 4 * (r >> 4) + (r & 3)
    return (((iota((16 * GROUPS, 128), 1) - target) & 127) == 0).astype(f32).astype(bf16)


def latitude_copies():
    source, lane = iota((64, 256), 0), iota((64, 256), 1)
    same = ((source >> 5) == (lane >> 7)) & ((source & 31) == (lane & 31))
    return same.astype(f32).astype(bf16)


def column_products(rows, order, copies):
    wide = dot(dot_nt(order, rows.astype(bf16)).astype(bf16), copies)
    own = ((iota(wide.shape, 1) >> 5) & 3) == (iota(wide.shape, 0) & 3)
    return jnp.where(own, wide, 0.0)


def slot_terms(shape, pair_first, slot_first):
    pair = pair_first + (iota(shape, 0) & 3)
    slot = slot_first + iota(shape, 1)
    upper = slot >= MT - pair
    odd = (jnp.where(upper, slot + pair, slot) & 1) == 1
    return pair, slot, upper, odd


def partial_solve(sums, pair_first, slot_first):
    shape = (8, sums.shape[1])
    pair, slot, upper, odd = slot_terms(shape, pair_first, slot_first)
    degree = jnp.where(upper, slot - 1, pair + slot)
    eigen = degree.astype(f32) * (degree + 1).astype(f32) / float(MT * MT)
    fields = []
    for field in range(3):
        block = [
            [sums[((par * 3 + field) * 2 + mem) * 8 :][:8] for mem in range(2)] for par in range(2)
        ]
        fields.append(
            jnp.where(
                upper,
                jnp.where(odd, block[1][1], block[0][1]),
                jnp.where(odd, block[1][0], block[0][0]),
            )
        )
    div_rhs = fields[1] - gravity_step * eigen * fields[2]
    height_spec = (fields[0] - time_step * div_rhs) / (1.0 + coupling * eigen)
    return height_spec, div_rhs + gravity_step * eigen * height_spec


def inverse_rows(solved, pair_first, slot_first):
    _, _, upper, odd = slot_terms(solved[0].shape, pair_first, slot_first)
    base = [x.astype(f32) for x in solved]
    rows = [jnp.where(upper, 0.0, x) for x in base] + [jnp.where(upper, x, 0.0) for x in base]
    rows += [jnp.where(odd, -x, x) for x in rows]
    return jnp.concatenate(rows, axis=0).astype(bf16)


def own_pair(products):
    lane = iota((HALF, 64), 1) & 3
    total = None
    for pair in range(GROUP):
        term = jnp.where(lane == pair, products[HALF * pair : HALF * (pair + 1)], 0.0)
        total = term if total is None else total + term
    return total


def lane_order(lon, group):
    r, c = iota((64, 512), 0), iota((64, 512), 1)
    member, part = (r >> 4) & 1, (r >> 2) & 1
    target = lon * PAIRS + 64 * part + 33 * member + 4 * group + (r & 3)
    same = ((r >> 5) == (c >> 8)) & (((r >> 3) & 1) == ((c >> 7) & 1))
    return (same & (((c - target) & 127) == 0)).astype(f32).astype(bf16)


def inverse_both(fields, spread_t, twist, back):
    mean = (iota((LON_DEV, 128), 0) == 0) & (iota((LON_DEV, 128), 1) == 0)
    total = None
    for member in range(2):
        straight, wrapped = lane_masks(member)
        turned = []
        for c in fields:
            stack = []
            for part in range(2):
                slot = part * 2 + member
                x = pltpu.roll(c, 128 - 32 * slot, 1) if slot else c
                if member == 0:
                    x = jnp.where(mean, 0.5 * x, x)
                stack += [jnp.where(straight, x, 0.0), jnp.where(wrapped, x, 0.0)]
            turned.append(jnp.concatenate(stack, axis=0).T)
        rows = slice(256 * member, 256 * (member + 1))
        b = three(dot, split(jnp.concatenate(turned, axis=0)), (back[0][rows], back[1][rows]))
        rows = slice(128 * member, 128 * (member + 1))
        cos, sin = twist[0][rows], twist[1][rows]
        z = [[], []]
        for f in range(2):
            re, im = b[128 * f : 128 * (f + 1), :256], b[128 * f : 128 * (f + 1), 256:]
            for part, x in enumerate((re * cos - im * sin, re * sin + im * cos)):
                z[part].append(x[:LON_DEV] + x[LON_DEV:])
        z = [jnp.concatenate(part, axis=1) for part in z]
        total = z if total is None else [total[0] + z[0], total[1] - z[1]]
    return three(dot, spread_t, split(jnp.concatenate(total, axis=0)))


CONSTS = 11
LAG = 1


def kernel(*refs):
    grid_in, refs = refs[:5], refs[5:]
    consts_in, refs = refs[:CONSTS], refs[CONSTS:]
    legendre, out, *refs = refs
    grid, refs = refs[:5], refs[5:]
    consts, refs = refs[:CONSTS], refs[CONSTS:]
    table, field_buf, row_buf, tx1, rx1, tx2, rx2, tx4, rx4, tx5, rx5, *refs = refs
    tails, order, copies, orders, columns, sums, sibling_sums, chip_tx, chip_rx, solved, message, *refs = refs
    in_sem, table_sem, send_sem, recv_sem, own_sem, lat_send, lat_recv = refs
    lon, lat = lax.axis_index("lon"), lax.axis_index("lat")
    core = lax.rem(lat, 2)
    sibling = {"lat": lat + 1 - 2 * core}
    across = {"lat": lax.rem(lat + 2, 4)}

    def peers(visit):
        x, z, y = lon >> 5, (lon >> 2) & 7, lon & 3
        for step in (4, 3, 5, 2, 6, 1, 7, 0):
            far = ((z + step) & 7) << 2

            def one(i, _):
                order = i >> 1
                turn = jnp.where(order == 0, 2, jnp.where(order == 1, 1, jnp.where(order == 2, 3, 0)))
                visit(((x ^ (1 - (i & 1))) << 5) | far | ((y + turn) & 3))
                return 0

            lax.fori_loop(0, 8 if step else 7, one, 0)

    def table_copy(g):
        rows = pl.ds(GROUP * g, GROUP)
        return pltpu.make_async_copy(legendre.at[rows], table.at[rows], table_sem.at[g])

    grid_copies = [
        pltpu.make_async_copy(a, b, in_sem.at[n]) for n, (a, b) in enumerate(zip(grid_in, grid))
    ]
    const_copies = [
        pltpu.make_async_copy(a, b, in_sem.at[5 + n])
        for n, (a, b) in enumerate(zip(consts_in, consts))
    ]
    for copy in grid_copies:
        copy.start()
    barrier = pltpu.get_barrier_semaphore()
    peers(lambda peer: pl.semaphore_signal(barrier, 1, device_id={"lon": peer}))
    pl.semaphore_signal(barrier, 1, device_id=sibling)
    pl.semaphore_signal(barrier, 1, device_id=across)
    for copy in const_copies:
        copy.start()
    for g in range(GROUPS):
        table_copy(g).start()

    def exchange_start(phase, tx, rx):
        n = tx.shape[0] // LON_DEV
        own = pl.ds(lon * n, n)
        peers(
            lambda peer: pltpu.make_async_remote_copy(
                tx.at[pl.ds(peer * n, n)],
                rx.at[own],
                send_sem.at[phase],
                recv_sem.at[phase],
                device_id={"lon": peer},
            ).start()
        )
        pltpu.make_async_copy(tx.at[own], rx.at[own], own_sem.at[phase]).start()

    def exchange_wait(phase, tx, rx):
        n = tx.shape[0] // LON_DEV
        own = pl.ds(lon * n, n)
        rest = pl.ds(0, (LON_DEV - 1) * n)
        pltpu.make_async_copy(tx.at[own], rx.at[own], own_sem.at[phase]).wait()
        pltpu.make_async_copy(rx.at[rest], rx.at[rest], recv_sem.at[phase]).wait()

    def exchange_sent(phase, tx):
        rest = pl.ds(0, (LON_DEV - 1) * (tx.shape[0] // LON_DEV))
        pltpu.make_async_copy(tx.at[rest], tx.at[rest], send_sem.at[phase]).wait()

    for copy in grid_copies:
        copy.wait()
    height, divergence, depth, tide, weight_row = grid
    weight = jnp.sum(
        jnp.where(
            iota((HALF, HALF), 0) == iota((HALF, HALF), 1),
            jnp.broadcast_to(weight_row[...], (HALF, HALF)),
            0.0,
        ),
        axis=1,
        keepdims=True,
    ) * (math.sqrt(NLON / NLAT) / MT / NLON)
    field_buf[...] = jnp.zeros_like(field_buf)
    fields = forcing_fields(height[...], divergence[...], depth[...], tide[...])
    for f in range(3):
        even, odd = fold(fields[f], weight)
        field_buf[0:HALF, 0:SPAN] = even
        field_buf[HALF:, 0:SPAN] = odd
        for h in range(2):
            row_buf[pl.ds(2 * f + h, LON_DEV, stride=6), :] = field_buf[:, 128 * h : 128 * (h + 1)]
    tx1[...] = row_buf[...].astype(bf16)

    pl.semaphore_wait(barrier, LON_DEV + 1)
    exchange_start(0, tx1, rx1)
    for copy in const_copies:
        copy.wait()
    spread, spread_t, twist, inner, back = (consts[n : n + 2] for n in (0, 2, 4, 6, 9))
    spread, spread_t = [r[...] for r in spread], [r[...] for r in spread_t]
    pick = consts[8]
    exchange_wait(0, tx1, rx1)

    row_buf[...] = rx1[...].astype(f32)
    x = jnp.concatenate([row_buf[pl.ds(c, LON_DEV, stride=6), :] for c in range(6)], axis=1)
    for f, rows in enumerate(forward_rows(x.astype(bf16), spread, twist, inner, pick)):
        tx2[pl.ds(f, LON_DEV, stride=3), :] = rows
    exchange_start(1, tx2, rx2)

    def prepare(g, _):
        table_copy(g).wait()
        last = table[pl.ds(GROUP * g, GROUP), :, SLOTS - 1 : SLOTS].reshape(128, 1).astype(f32)
        last = jnp.where(iota((128, 128), 1) == 0, jnp.broadcast_to(last, (128, 128)), 0.0)
        tails[g] = last.astype(bf16)
        orders[g] = lane_order(lon, g)
        return 0

    lax.fori_loop(0, GROUPS, prepare, 0)
    order[...] = pair_order(lon)
    copies[...] = latitude_copies()
    message[...] = jnp.zeros_like(message)
    exchange_wait(1, tx2, rx2)

    for f in range(3):
        rows = rx2[pl.ds(f, LON_DEV, stride=3), :]
        wide = column_products(rows, order[...], copies[...]).astype(bf16)
        for g in range(GROUPS):
            for par in range(2):
                columns[g, 16 * (par * 3 + f) : 16 * (par * 3 + f + 1), :] = wide[
                    16 * g : 16 * (g + 1), 128 * par : 128 * (par + 1)
                ]

    def table_tile(g, t):
        return table[pl.ds(GROUP * g, GROUP), :, TILE * t : TILE * (t + 1)].reshape(128, TILE)

    def tiles(g):
        for t in range(TILES):
            yield TILE * t, TILE, table_tile(g, t)
        yield TILE * TILES, 128, tails[g]

    def sibling_copy(g):
        return pltpu.make_async_remote_copy(
            sums.at[g, 1 - core],
            sibling_sums.at[g],
            lat_send.at[0, g],
            lat_recv.at[0, g],
            device_id=sibling,
        )

    def across_copy(g):
        return pltpu.make_async_remote_copy(
            chip_tx.at[g], chip_rx.at[g], lat_send.at[1, g], lat_recv.at[1, g], device_id=across
        )

    def share_copy(g):
        return pltpu.make_async_remote_copy(
            solved.at[g, core],
            solved.at[g, core],
            lat_send.at[2, g],
            lat_recv.at[2, g],
            device_id=sibling,
        )

    def forward_group(g):
        pair_first = lon * PAIRS + GROUP * g
        for first, width, rhs in tiles(g):
            both = partial_solve(dot(columns[g], rhs), pair_first, first)
            for field in range(2):
                sums[g, field, :, first : first + width] = both[field]
        sibling_copy(g).start()

    def sibling_sum(g):
        sibling_copy(g).wait_recv()
        total = sums[g, core] + sibling_sums[g]
        chip_tx[g] = total.astype(bf16)
        across_copy(g).start()
        sibling_sums[g] = total

    def across_sum(g):
        across_copy(g).wait_recv()
        total = sibling_sums[g] + chip_rx[g].astype(f32)
        solved[g, core] = total.astype(bf16)
        share_copy(g).start()

    def inverse_group(g):
        share_copy(g).wait_recv()
        pair_first = lon * PAIRS + GROUP * g
        total = None
        for first, width, rhs in tiles(g):
            both = [solved[g, field, :, first : first + width] for field in range(2)]
            term = dot_nt(rhs, inverse_rows(both, pair_first, first))
            total = term if total is None else total + term
        high, low = split(own_pair(total))
        message[...] += dot(high, orders[g]) + dot(low, orders[g])

    def forward_step(t, _):
        forward_group(t)

        @pl.when(t >= LAG)
        def _():
            sibling_sum(t - LAG)

        return 0

    lax.fori_loop(0, GROUPS, forward_step, 0)
    for g in range(GROUPS - LAG, GROUPS):
        sibling_sum(g)

    across_sum(0)

    def inverse_step(t, _):
        @pl.when(t + 1 < GROUPS)
        def _():
            across_sum(t + 1)

        inverse_group(t)
        return 0

    lax.fori_loop(0, GROUPS, inverse_step, 0)

    for field in range(2):
        for side in range(2):
            tx4[pl.ds(2 * HALF * side + field, HALF, stride=2), :] = message[
                :, 128 * (2 * side + field) : 128 * (2 * side + field + 1)
            ]
    exchange_start(2, tx4, rx4)
    exchange_wait(2, tx4, rx4)

    fields = [rx4[pl.ds(field, LON_DEV, stride=2), :] for field in range(2)]
    grid = inverse_both(fields, spread_t, twist, back)
    for c in range(4):
        tx5[pl.ds(c, LON_DEV, stride=4), :] = grid[:, 128 * c : 128 * (c + 1)]
    exchange_start(3, tx5, rx5)
    exchange_wait(3, tx5, rx5)
    for field in range(2):
        for h in range(2):
            out[field, :, 128 * h : 128 * (h + 1)] = rx5[pl.ds(2 * field + h, LON_DEV, stride=4), :]

    for phase, tx in enumerate((tx1, tx2, tx4, tx5)):
        exchange_sent(phase, tx)
    for g in range(GROUPS):
        for copy in (sibling_copy, across_copy, share_copy):
            copy(g).wait_send()


def per_device(height, divergence, depth, tide, gauss_weight, legendre):
    consts = [jnp.asarray(t) for t in tables()]
    grid = (height, divergence, depth, tide, gauss_weight.reshape(1, HALF))
    vmem, hbm = pl.BlockSpec(memory_space=pltpu.VMEM), pl.BlockSpec(memory_space=pltpu.HBM)
    grid_shape = jax.ShapeDtypeStruct(height.shape, f32)

    def pair(rows, dtype=f32):
        return [pltpu.VMEM((LON_DEV * rows, 128), dtype)] * 2

    wide = 128 * pl.cdiv(SLOTS, 128)
    raw = pl.pallas_call(
        kernel,
        out_shape=jax.ShapeDtypeStruct((2, LON_DEV, 256), f32),
        in_specs=[hbm] * (len(grid) + len(consts) + 1),
        out_specs=vmem,
        scratch_shapes=[
            *[pltpu.VMEM(x.shape, x.dtype) for x in (*grid, *consts)],
            pltpu.VMEM((PAIRS, HALF, SLOTS), bf16),
            pltpu.VMEM((2 * HALF, 256), f32),
            pltpu.VMEM((LON_DEV * 6, 128), f32),
            *pair(6, bf16),
            *pair(3),
            *pair(2),
            *pair(4),
            pltpu.VMEM((GROUPS, 128, 128), bf16),
            pltpu.VMEM((16 * GROUPS, 128), bf16),
            pltpu.VMEM((2 * HALF, 256), bf16),
            pltpu.VMEM((GROUPS, 64, 512), bf16),
            pltpu.VMEM((GROUPS, 96, 128), bf16),
            pltpu.VMEM((GROUPS, 2, 8, wide), f32),
            pltpu.VMEM((GROUPS, 8, wide), f32),
            pltpu.VMEM((GROUPS, 8, wide), bf16),
            pltpu.VMEM((GROUPS, 8, wide), bf16),
            pltpu.VMEM((GROUPS, 2, 8, wide), bf16),
            pltpu.VMEM((HALF, 512), f32),
            pltpu.SemaphoreType.DMA((5 + CONSTS,)),
            pltpu.SemaphoreType.DMA((GROUPS,)),
            pltpu.SemaphoreType.DMA((4,)),
            pltpu.SemaphoreType.DMA((4,)),
            pltpu.SemaphoreType.DMA((4,)),
            pltpu.SemaphoreType.DMA((3, GROUPS)),
            pltpu.SemaphoreType.DMA((3, GROUPS)),
        ],
        compiler_params=pltpu.CompilerParams(
            collective_id=0, has_side_effects=True, vmem_limit_bytes=48 << 20
        ),
    )(*[pltpu.with_memory_space_constraint(x, pltpu.HBM) for x in (*grid, *consts, legendre)])
    return raw[0, :, :SPAN], raw[1, :, :SPAN]


def solution(mesh):
    in_specs = (
        P("lat", "lon"),
        P("lat", "lon"),
        P("lat", "lon"),
        P("lat", "lon"),
        P("lat"),
        P("lon", "lat", None),
    )
    out_specs = (P("lat", "lon"), P("lat", "lon"))
    return jax.shard_map(
        per_device, mesh=mesh, in_specs=in_specs, out_specs=out_specs, check_vma=False
    )
```
